256 devices in a mesh: grp: 8 (over x_hi, y), blk: 32 (over x_lo, z, core).
Axes of the slice: x: 4 (x_hi: 2, x_lo: 2; x = x_hi * 2 + x_lo), y: 4, z: 8, core: 2. Of those that a mesh axis runs over, the one named last changes fastest.
Arguments:
- queries: bfloat16 [32768, 4096], P(('grp', 'blk')), parts along dimension 0, may hold values from -256 to 256
- new_keys: bfloat16 [32768, 512], P(('grp', 'blk')), parts along dimension 0, may hold values from -6 to 6
- new_values: bfloat16 [32768, 512], P(('grp', 'blk')), parts along dimension 0, may hold values from -6 to 6
- prefix_keys: bfloat16 [32768, 512], P(('grp', 'blk')), parts along dimension 0, may hold values from -6 to 6
- prefix_values: bfloat16 [32768, 512], P(('grp', 'blk')), parts along dimension 0, may hold values from -6 to 6
- block_table: int32 [256, 16], P(('grp', 'blk')), parts along dimension 0, may hold values from 0 to 31, as said below
- prefix_blocks: int32 [256], P(('grp', 'blk')), parts along dimension 0, may hold values from 1 to 16, 320 in all
Outputs:
- attended: bfloat16 [32768, 4096], P(('grp', 'blk')), parts along dimension 0
The draws below stay inside these ranges and needn't reach their ends.
There are 8 independent parts, one for each index of `grp`. The reference program is written for one: setup_inputs(seed, part) draws one part's arguments, and reference() takes and returns one part's arrays. A program takes and returns all parts, laid end to end along the dimension named above; each array names one. Nothing has to cross between parts.
Inputs may be any that keep to these rules, and one draw needn't show every extreme that they name: `block_table`: each row names 16 different prefix blocks; only the first prefix_blocks entries of a row are read. `prefix_blocks`: within each group (each index of grp) the lengths sum to 320.
All inputs are finite; a program needn't handle non-finite values.
Results may differ from the reference program's by a relative error of at most 0.008.
Values may be sent and summed in bfloat16 or wider, within the bound.
No kernel may reach another device: no remote copies, remote signals or barrier semaphores. Data moves between devices by JAX's collectives and lax.ppermute only.
A program may use at most 64 MiB of HBM per device.

```python
import math
import jax
import jax.numpy as jnp
import numpy as np
from jax import lax

H = 32
KVH = 4
DH = 128
BS = 128
NEW = 128
G = 8
REQUESTS = 32
POOL_BLOCKS = 32
MAXB = 16


def table_rows(key):
    row_keys = jax.random.split(jax.random.fold_in(key, 11), REQUESTS)
    return jax.vmap(lambda one: jax.random.permutation(one, POOL_BLOCKS)[:MAXB])(row_keys).astype(jnp.int32)


def key_field(key):
    base = jax.random.truncated_normal(jax.random.fold_in(key, 23), -6.0, 6.0, (POOL_BLOCKS, BS, KVH * DH), jnp.float32)
    return base


def draw_block_table(key, part):
    return table_rows(key)


def draw_prefix_keys(key, part):
    return key_field(key).reshape(POOL_BLOCKS * BS, KVH * DH).astype(jnp.bfloat16)


def draw_queries(key, part):
    base = jax.random.truncated_normal(jax.random.fold_in(key, 29), -6.0, 6.0, (REQUESTS, NEW, H * DH), jnp.float32)
    return base.reshape(REQUESTS * NEW, H * DH).astype(jnp.bfloat16)


def level_of(own_key, shape, pieces, low, high):
    def one(dim, parts):
        draws = jax.random.uniform(jax.random.fold_in(jax.random.fold_in(own_key, 6), dim), (parts,), jnp.float32, low / len(pieces), high / len(pieces))
        return jnp.repeat(jnp.exp(draws), shape[dim] // parts).reshape((-1,) + (1,) * (len(shape) - dim - 1))

    factor_of = one(*pieces[0])
    for cut in pieces[1:]:
        factor_of = factor_of * one(*cut)
    return factor_of


def length_profile(count, total, limit, lean):
    loads = [(1 << 20) // math.isqrt(standing ** lean) + 1 for standing in range(2, count + 1)]
    surplus, given = total - limit - (count - 1), [1] * (count - 1)
    while surplus > 0:
        candidates = [i for i in range(count - 1) if given[i] < limit]
        pool, remaining = sum([loads[i] for i in candidates]), surplus
        for i in candidates:
            addition = min(limit - given[i], max(1, remaining * loads[i] // pool), surplus)
            given[i] = given[i] + addition
            surplus = surplus - addition
    return np.array([limit] + given)


def ragged(key, count, total, reach, skew):
    if count == 2:
        one = jax.random.randint(key, (), max(1, total - reach), min(reach, total - 1) + 1)
        return jnp.stack([one, total - one])
    tallies = jnp.asarray(length_profile(count, total, reach, skew), jnp.int32)
    twos = (count - 1) // 2
    giver, receiver = tallies[1:1 + 2 * twos:2], tallies[2:2 + 2 * twos:2]
    slack = jnp.minimum(giver - 1, reach - receiver)
    passed = jax.random.randint(jax.random.fold_in(key, 1), (twos,), 0, 1 << 20) % (slack + 1)
    tallies = tallies.at[1:1 + 2 * twos:2].set(giver - passed).at[2:2 + 2 * twos:2].set(receiver + passed)
    return tallies[jax.random.permutation(jax.random.fold_in(key, 2), count)]


def normal_values(key, shape, scale, limit, cuts=(), held_as=jnp.bfloat16):
    loudness = level_of(key, shape, cuts, -0.22, 0.18) if cuts else 1.0
    values = jax.random.normal(key, shape, jnp.float32) * scale * loudness
    return jnp.minimum(jnp.maximum(values, -limit), limit).astype(held_as)


def setup_inputs(seed: int = 0, part: int = 0) -> dict:
    key_list = jax.random.split(jax.random.key(seed), 8)
    part_keys = jax.random.split(jax.random.fold_in(key_list[7], part), 8)
    queries = draw_queries(jax.random.fold_in(jax.random.fold_in(key_list[7], part), 71), part)
    new_keys = normal_values(part_keys[1], (REQUESTS * NEW, KVH * DH), 1.0, 6.0, ((0, 32),))
    new_values = normal_values(part_keys[2], (REQUESTS * NEW, KVH * DH), 1.0, 6.0, ((0, 32),))
    prefix_keys = draw_prefix_keys(jax.random.fold_in(jax.random.fold_in(key_list[7], part), 71), part)
    prefix_values = normal_values(part_keys[4], (POOL_BLOCKS * BS, KVH * DH), 1.0, 6.0, ((0, 32),))
    block_table = draw_block_table(jax.random.fold_in(jax.random.fold_in(key_list[7], part), 71), part)
    prefix_blocks = ragged(part_keys[6], REQUESTS, REQUESTS * MAXB * 5 // 8, MAXB, 1).astype(jnp.int32)
    return dict(queries=queries, new_keys=new_keys, new_values=new_values, prefix_keys=prefix_keys, prefix_values=prefix_values, block_table=block_table, prefix_blocks=prefix_blocks)


def reference(queries, new_keys, new_values, prefix_keys, prefix_values, block_table, prefix_blocks):
    scale = DH ** -0.5
    pool_keys = prefix_keys.reshape(POOL_BLOCKS, BS, KVH * DH)
    pool_values = prefix_values.reshape(POOL_BLOCKS, BS, KVH * DH)
    span = MAXB * BS + NEW
    position = jnp.arange(span, dtype=jnp.int32)
    token = jnp.arange(NEW, dtype=jnp.int32)

    def one_request(items):
        query, nkey, nvalue, row, length = items
        keys = jnp.concatenate([jnp.take(pool_keys, row, axis=0).reshape(MAXB * BS, KVH * DH), nkey], axis=0)
        values = jnp.concatenate([jnp.take(pool_values, row, axis=0).reshape(MAXB * BS, KVH * DH), nvalue], axis=0)
        qf = query.astype(jnp.float32).reshape(NEW, KVH, G, DH)
        kf = keys.astype(jnp.float32).reshape(span, KVH, DH)
        vf = values.astype(jnp.float32).reshape(span, KVH, DH)
        scores = jnp.einsum("nkgd,lkd->kgnl", qf, kf) * scale
        before = (position < MAXB * BS) & (position // BS < length)
        causal = (position[None, :] >= MAXB * BS) & (position[None, :] - MAXB * BS <= token[:, None])
        visible = before[None, :] | causal
        scores = jnp.where(visible[None, None], scores, -jnp.inf)
        top = jnp.max(scores, axis=-1, keepdims=True)
        weights = jnp.exp(scores - top)
        total = jnp.sum(weights, axis=-1)
        rounded = lax.optimization_barrier(weights.astype(jnp.bfloat16)).astype(jnp.float32)
        summed = jnp.einsum("kgnl,lkd->nkgd", rounded, vf)
        result = summed / jnp.transpose(total, (2, 0, 1))[..., None]
        return result.reshape(NEW, H * DH).astype(jnp.bfloat16)

    outputs = lax.map(one_request, (queries.reshape(REQUESTS, NEW, H * DH), new_keys.reshape(REQUESTS, NEW, KVH * DH), new_values.reshape(REQUESTS, NEW, KVH * DH), block_table.astype(jnp.int32), prefix_blocks.astype(jnp.int32)))
    return outputs.reshape(REQUESTS * NEW, H * DH)
```

```python
import functools
import math

import jax
import jax.numpy as jnp
from jax import lax
from jax.experimental import pallas as pl
from jax.experimental.pallas import tpu as pltpu
from jax.sharding import PartitionSpec as P

H = 32
KVH = 4
DH = 128
BS = 128
G = 8
KW = KVH * DH
CHUNK = 4
MAXB = 16
CAP = MAXB + CHUNK
ROWS = 256
HEADS = ROWS // BS
SCALE = DH**-0.5 * math.log2(math.e)


def index(x, z, c):
    return ((x % 2) * 8 + z % 8) * 2 + c % 2


def pairs(target):
    return [
        (index(x, z, c), index(*target(x, z, c)))
        for x in range(2)
        for z in range(8)
        for c in range(2)
    ]


AHEAD = pairs(lambda x, z, c: (x, z + 1 - 2 * c, c))
BACK = pairs(lambda x, z, c: (x, z - 1 + 2 * c, c))
ACROSS = pairs(lambda x, z, c: (x + 1, z, c))
SIBLING = pairs(lambda x, z, c: (x, z, c + 1))


def send(piece, table):
    return lax.ppermute(piece, "blk", table)


def gather(piece):
    x0 = send(piece, ACROSS)
    a1, b1 = send(piece, AHEAD), send(piece, BACK)
    a2, b2 = send(a1, AHEAD), send(b1, BACK)
    xa1, xb1 = send(x0, AHEAD), send(x0, BACK)
    xa2, xb2 = send(a2, ACROSS), send(b2, ACROSS)
    a3, b3 = send(a2, AHEAD), send(b2, BACK)
    xb3, xa3 = send(xb2, BACK), send(a3, ACROSS)
    a4 = send(a3, AHEAD)
    xa4 = send(a4, ACROSS)
    held = [
        (piece, 0, 0), (x0, 1, 0),
        (a1, 0, -1), (b1, 0, 1), (xa1, 1, -1), (xb1, 1, 1),
        (a2, 0, -2), (b2, 0, 2), (xa2, 1, -2), (xb2, 1, 2),
        (a3, 0, -3), (b3, 0, 3), (xa3, 1, -3), (xb3, 1, 3),
        (a4, 0, -4), (xa4, 1, -4),
    ]
    me = lax.axis_index("blk")
    x, z, c = me // 16, (me // 2) % 8, me % 2
    way = 1 - 2 * c
    pieces, owners = [], []
    for array, dx, dz in held:
        pieces.append(array)
        owners.append((((x + dx) % 2) * 8 + (z + dz * way) % 8) * 2 + c)
        pieces.append(send(array, SIBLING))
        owners.append((((x + dx) % 2) * 8 + (z - dz * way) % 8) * 2 + 1 - c)
    return pieces, jnp.stack(owners)


def attend(slots, used_ref, place_ref, count_ref, q_ref, nk_ref, nv_ref, *rest):
    pieces = rest[:slots]
    out_ref, kv_ref, acc_ref, top_ref, sems = rest[slots:]
    count = count_ref[0]

    for i in range(slots):
        @pl.when(used_ref[i] > 0)
        def _(i=i):
            pltpu.make_async_copy(pieces[i], kv_ref.at[place_ref[i]], sems.at[i]).start()

    ones = jnp.ones((BS, DH), jnp.bfloat16)
    many = jnp.ones((CHUNK * BS, DH), jnp.bfloat16)
    row = lax.broadcasted_iota(jnp.int32, (ROWS, BS), 0) % BS
    causal = lax.broadcasted_iota(jnp.int32, (ROWS, BS), 1) <= row
    lane = lax.broadcasted_iota(jnp.int32, (ROWS, CHUNK * BS), 1)
    groups = G // HEADS

    def query(t):
        first = t * HEADS
        return jnp.concatenate(
            [q_ref[:, pl.ds(pl.multiple_of((first + j) * DH, DH), DH)] for j in range(HEADS)], axis=0
        )

    def dot_t(a, b):
        return lax.dot_general(a, b, (((1,), (1,)), ((), ())), preferred_element_type=jnp.float32)

    @pl.loop(0, H // HEADS)
    def _(t):
        g = t // groups
        col = pl.ds(pl.multiple_of(g * DH, DH), DH)
        s = jnp.where(causal, dot_t(query(t), nk_ref[:, col]) * SCALE, -jnp.inf)
        top = jnp.max(s, axis=1, keepdims=True)
        w = jnp.exp2(s - top).astype(jnp.bfloat16)
        rhs = jnp.concatenate([nv_ref[:, col], ones], axis=1)
        rows = pl.ds(pl.multiple_of(t * ROWS, ROWS), ROWS)
        acc_ref[rows, :] = jnp.dot(w, rhs, preferred_element_type=jnp.float32)
        top_ref[rows, :] = jnp.broadcast_to(top, (ROWS, DH))

    for i in range(slots):
        @pl.when(used_ref[i] > 0)
        def _(i=i):
            pltpu.make_async_copy(pieces[i], kv_ref.at[place_ref[i]], sems.at[i]).wait()

    for j in range(CHUNK - 1):
        kv_ref[count + j, :, KW:] = jnp.zeros((BS, KW), jnp.bfloat16)

    @pl.loop(0, (count + CHUNK - 1) // CHUNK)
    def _(k):
        live = (count - k * CHUNK) * BS
        blocks = pl.ds(k * CHUNK, CHUNK)

        @pl.loop(0, H // HEADS)
        def _(t):
            g = t // groups
            rows = pl.ds(pl.multiple_of(t * ROWS, ROWS), ROWS)
            key = kv_ref[blocks, :, pl.ds(pl.multiple_of(g * DH, DH), DH)].reshape(CHUNK * BS, DH)
            value = kv_ref[blocks, :, pl.ds(pl.multiple_of(KW + g * DH, DH), DH)].reshape(CHUNK * BS, DH)
            s = jnp.where(lane < live, dot_t(query(t), key) * SCALE, -jnp.inf)
            old = top_ref[rows, :]
            top = jnp.maximum(old, jnp.max(s, axis=1, keepdims=True))
            factor = jnp.exp2(old - top)
            w = jnp.exp2(s - jnp.tile(top, (1, CHUNK))).astype(jnp.bfloat16)
            rhs = jnp.concatenate([value, many], axis=1)
            acc_ref[rows, :] = acc_ref[rows, :] * jnp.tile(factor, (1, 2)) + jnp.dot(
                w, rhs, preferred_element_type=jnp.float32
            )
            top_ref[rows, :] = top

    @pl.loop(0, H // HEADS)
    def _(t):
        for j in range(HEADS):
            rows = pl.ds(pl.multiple_of(t * ROWS + j * BS, BS), BS)
            total = acc_ref[rows, DH:]
            out_ref[:, pl.ds(pl.multiple_of((t * HEADS + j) * DH, DH), DH)] = (
                acc_ref[rows, :DH] / total
            ).astype(jnp.bfloat16)


def body(queries, new_keys, new_values, prefix_keys, prefix_values, block_table, prefix_blocks):
    piece = jnp.concatenate([prefix_keys, prefix_values], axis=1)
    pieces, owners = gather(piece)
    slots = len(pieces)
    live = jnp.arange(MAXB, dtype=jnp.int32) < prefix_blocks[0]
    used = jnp.any((block_table[0][None, :] == owners[:, None]) & live[None, :], axis=1).astype(jnp.int32)
    order = jnp.arange(slots, dtype=jnp.int32)
    place = jnp.sum(jnp.where(order[None, :] < order[:, None], used[None, :], 0), axis=1)
    count = jnp.sum(used)[None]
    vmem = pl.BlockSpec(memory_space=pltpu.VMEM)
    smem = pl.BlockSpec(memory_space=pltpu.SMEM)
    return pl.pallas_call(
        functools.partial(attend, slots),
        out_shape=jax.ShapeDtypeStruct(queries.shape, jnp.bfloat16),
        in_specs=[smem] * 3 + [vmem] * 3 + [pl.BlockSpec(memory_space=pl.ANY)] * slots,
        out_specs=vmem,
        scratch_shapes=[
            pltpu.VMEM((CAP, BS, 2 * KW), jnp.bfloat16),
            pltpu.VMEM((H * BS, 2 * DH), jnp.float32),
            pltpu.VMEM((H * BS, DH), jnp.float32),
            pltpu.SemaphoreType.DMA((slots,)),
        ],
        compiler_params=pltpu.CompilerParams(vmem_limit_bytes=40 << 20),
    )(used, place, count, queries, new_keys, new_values, *pieces)


def solution(mesh):
    spec = P(("grp", "blk"), None)
    return jax.shard_map(
        body, mesh=mesh, in_specs=(spec,) * 6 + (P(("grp", "blk")),), out_specs=spec, check_vma=False
    )
```

```python
import functools
import math

import jax
import jax.numpy as jnp
from jax import lax
from jax.experimental import pallas as pl
from jax.experimental.pallas import tpu as pltpu
from jax.sharding import PartitionSpec as P

KVH = 4
DH = 128
BS = 128
G = 8
GW = G * DH
ROWS = G * BS
CHUNK = 4
MAXB = 16
CHUNKS = MAXB // CHUNK
MSG = GW + 3 * DH
PLANE = 4
DEPTH = 8
SCALE = DH**-0.5 * math.log2(math.e)


def index(x, z, c):
    return ((x % 2) * 8 + z % 8) * 2 + c % 2


def pairs(target):
    return [
        (index(x, z, c), index(*target(x, z, c)))
        for x in range(2)
        for z in range(8)
        for c in range(2)
    ]


AHEAD = pairs(lambda x, z, c: (x, z + 1 - 2 * c, c))
BACK = pairs(lambda x, z, c: (x, z - 1 + 2 * c, c))
SIBLING = pairs(lambda x, z, c: (x, z, c + 1))
ACROSS = pairs(lambda x, z, c: (x + 1, z, c))
DIAGONAL = pairs(lambda x, z, c: (x + 1, z, c + 1))
PEERS = (SIBLING, ACROSS, DIAGONAL)

VMEM = pl.BlockSpec(memory_space=pltpu.VMEM)
SMEM = pl.BlockSpec(memory_space=pltpu.SMEM)
ANY = pl.BlockSpec(memory_space=pl.ANY)


def send(piece, table):
    return lax.ppermute(piece, "blk", table)


def column(start, size):
    return pl.ds(pl.multiple_of(start * size, size), size)


def pack_pool(head_ref, k_ref, v_ref, *outs):
    for j in range(PLANE):
        head = head_ref[j]
        outs[j][:, :DH] = k_ref[:, column(head, DH)]
        outs[j][:, DH:] = v_ref[:, column(head, DH)]


def pack_request(head_ref, q_ref, k_ref, v_ref, meta_ref, *outs):
    for j in range(PLANE):
        head = head_ref[j]
        outs[j][:, :GW] = q_ref[:, column(head, GW)]
        outs[j][:, GW : GW + DH] = k_ref[:, column(head, DH)]
        outs[j][:, GW + DH : GW + 2 * DH] = v_ref[:, column(head, DH)]
        outs[j][:, GW + 2 * DH :] = meta_ref[...]


def assemble(head_ref, *refs):
    parts, out_ref, sems = refs[:PLANE], refs[PLANE], refs[PLANE + 1]
    copies = [
        pltpu.make_async_copy(parts[j], out_ref.at[:, column(head_ref[j], GW)], sems.at[j])
        for j in range(PLANE)
    ]
    for copy in copies:
        copy.start()
    for copy in copies:
        copy.wait()


def attend(slot_ref, length_ref, *refs):
    msgs, pieces, outs = refs[:2], refs[2 : 2 + DEPTH], refs[2 + DEPTH : 4 + DEPTH]
    kv_ref, qs_ref, s_ref, own_ref, top_ref, acc_ref, sems = refs[4 + DEPTH :]
    copies = [
        pltpu.make_async_copy(pieces[i], kv_ref.at[pl.ds(i * PLANE, PLANE)], sems.at[i])
        for i in range(DEPTH)
    ]
    for copy in copies:
        copy.start()
    row = lax.broadcasted_iota(jnp.int32, (ROWS, BS), 0) % BS
    causal = lax.broadcasted_iota(jnp.int32, (ROWS, BS), 1) <= row
    ones = jnp.ones((BS, DH), jnp.bfloat16)
    count = [(length_ref[r] + CHUNK - 1) // CHUNK for r in range(2)]

    def scores(r, keys):
        return (
            lax.dot_general(
                qs_ref[r], keys, (((1,), (1,)), ((), ())), preferred_element_type=jnp.float32
            )
            * SCALE
        )

    def own_scores(r):
        for h in range(G):
            qs_ref[r, h * BS : (h + 1) * BS, :] = msgs[r][:, h * DH : (h + 1) * DH]
        s = jnp.where(causal, scores(r, msgs[r][:, GW : GW + DH]), -jnp.inf)
        own_ref[r] = s
        top_ref[r] = s

    def entry(r, k, j):
        at = k * CHUNK + j
        live = at < length_ref[r]
        return slot_ref[r, jnp.where(live, at, 0)], live

    def chunk_scores(r, k):
        keys = jnp.concatenate([kv_ref[entry(r, k, j)[0], :, :DH] for j in range(CHUNK)], axis=0)
        s = scores(r, keys)
        s_ref[r, k] = s
        top = top_ref[r]
        for j in range(CHUNK):
            top = jnp.maximum(top, s[:, j * BS : (j + 1) * BS])
        top_ref[r] = top

    def own_values(r):
        top = jnp.broadcast_to(jnp.max(top_ref[r], axis=1, keepdims=True), (ROWS, BS))
        top_ref[r] = top
        w = jnp.exp2(own_ref[r] - top).astype(jnp.bfloat16)
        rhs = jnp.concatenate([msgs[r][:, GW + DH : GW + 2 * DH], ones], axis=1)
        acc_ref[...] = jnp.dot(w, rhs, preferred_element_type=jnp.float32)

    def chunk_values(r, k):
        w = jnp.exp2(s_ref[r, k] - jnp.tile(top_ref[r], (1, CHUNK))).astype(jnp.bfloat16)
        rhs = []
        for j in range(CHUNK):
            slot, live = entry(r, k, j)
            both = jnp.concatenate([kv_ref[slot, :, DH:], ones], axis=1)
            rhs.append(jnp.where(live, both, jnp.zeros_like(both)))
        acc_ref[...] += jnp.dot(w, jnp.concatenate(rhs, axis=0), preferred_element_type=jnp.float32)

    def finish(r):
        for h in range(G):
            a = acc_ref[h * BS : (h + 1) * BS, :]
            outs[r][:, h * DH : (h + 1) * DH] = (a[:, :DH] / a[:, DH:]).astype(jnp.bfloat16)

    own_scores(0)
    for copy in copies:
        copy.wait()

    @pl.loop(0, count[0])
    def _(k):
        chunk_scores(0, k)

    own_values(0)
    own_scores(1)
    both = jnp.minimum(count[0], count[1])

    @pl.loop(0, both)
    def _(k):
        chunk_values(0, k)
        chunk_scores(1, k)

    @pl.loop(both, count[0])
    def _(k):
        chunk_values(0, k)

    @pl.loop(both, count[1])
    def _(k):
        chunk_scores(1, k)

    finish(0)
    own_values(1)

    @pl.loop(0, count[1])
    def _(k):
        chunk_values(1, k)

    finish(1)


def run_attend(slots, lengths, msgs, pieces):
    part = jax.ShapeDtypeStruct((BS, GW), jnp.bfloat16)
    return pl.pallas_call(
        attend,
        out_shape=(part, part),
        in_specs=[SMEM] * 2 + [VMEM] * 2 + [ANY] * DEPTH,
        out_specs=(VMEM, VMEM),
        scratch_shapes=[
            pltpu.VMEM((PLANE * DEPTH, BS, 2 * DH), jnp.bfloat16),
            pltpu.VMEM((2, ROWS, DH), jnp.bfloat16),
            pltpu.VMEM((2, CHUNKS, ROWS, CHUNK * BS), jnp.float32),
            pltpu.VMEM((2, ROWS, BS), jnp.float32),
            pltpu.VMEM((2, ROWS, BS), jnp.float32),
            pltpu.VMEM((ROWS, 2 * DH), jnp.float32),
            pltpu.SemaphoreType.DMA((DEPTH,)),
        ],
        cost_estimate=pl.CostEstimate(flops=2800000000, bytes_accessed=4 << 20, transcendentals=4 << 20),
        compiler_params=pltpu.CompilerParams(vmem_limit_bytes=36 << 20),
    )(slots, lengths, *msgs, *pieces)


def body(queries, new_keys, new_values, prefix_keys, prefix_values, block_table, prefix_blocks):
    me = lax.axis_index("blk")
    x, z, c = me // 16, (me // 2) % 8, me % 2
    heads = jnp.stack([2 * x + c, 2 * x + 1 - c, 2 * (1 - x) + c, 2 * (1 - x) + 1 - c]).astype(jnp.int32)

    shard = jax.ShapeDtypeStruct((BS, 2 * DH), jnp.bfloat16)
    own, *outgoing = pl.pallas_call(
        pack_pool, out_shape=(shard,) * PLANE, in_specs=[SMEM, VMEM, VMEM], out_specs=(VMEM,) * PLANE
    )(heads, prefix_keys, prefix_values)
    piece = jnp.stack([own] + [send(o, t) for o, t in zip(outgoing, PEERS)])

    meta = jnp.concatenate([block_table[0], prefix_blocks]).astype(jnp.bfloat16)
    meta = jnp.broadcast_to(jnp.pad(meta, (0, DH - MAXB - 1))[None], (BS, DH))
    shard = jax.ShapeDtypeStruct((BS, MSG), jnp.bfloat16)
    own, *outgoing = pl.pallas_call(
        pack_request, out_shape=(shard,) * PLANE, in_specs=[SMEM] + [VMEM] * 4, out_specs=(VMEM,) * PLANE
    )(heads, queries, new_keys, new_values, meta)
    msgs = [own] + [send(o, t) for o, t in zip(outgoing, PEERS)]

    a, b = [piece], [piece]
    for step in range(4):
        a.append(send(a[-1], AHEAD))
        if step < 3:
            b.append(send(b[-1], BACK))
    pieces = b + a[:0:-1]

    info = jnp.stack([m[0, GW + 2 * DH : GW + 2 * DH + MAXB + 1] for m in msgs]).astype(jnp.int32)
    table, lengths = info[:, :MAXB], info[:, MAXB]
    deep = (((table // 2) % 8 - z) * (1 - 2 * c)) % 8
    slots = deep * 4 + (table // 16 ^ x) * 2 + (table % 2 ^ c)

    far = run_attend(slots[2:], lengths[2:], msgs[2:], pieces)
    near = run_attend(slots[:2], lengths[:2], msgs[:2], pieces)
    parts = [near[0], send(near[1], SIBLING), send(far[0], ACROSS), send(far[1], DIAGONAL)]
    return pl.pallas_call(
        assemble,
        out_shape=jax.ShapeDtypeStruct(queries.shape, jnp.bfloat16),
        in_specs=[SMEM] + [VMEM] * PLANE,
        out_specs=ANY,
        scratch_shapes=[pltpu.SemaphoreType.DMA((PLANE,))],
    )(heads, *parts)


def solution(mesh):
    spec = P(("grp", "blk"), None)
    return jax.shard_map(
        body, mesh=mesh, in_specs=(spec,) * 6 + (P(("grp", "blk")),), out_specs=spec, check_vma=False
    )
```

```python
import functools
import math

import jax
import jax.numpy as jnp
from jax import lax
from jax.experimental import pallas as pl
from jax.experimental.pallas import tpu as pltpu
from jax.sharding import PartitionSpec as P

KVH = 4
DH = 128
BS = 128
G = 8
GW = G * DH
ROWS = G * BS
CHUNK = 4
MAXB = 16
CHUNKS = MAXB // CHUNK
MSG = GW + 3 * DH
PLANE = 4
DEPTH = 8
PIECES = 2 * DEPTH
HALF = PLANE // 2
SCALE = DH**-0.5 * math.log2(math.e)


def index(x, z, c):
    return ((x % 2) * 8 + z % 8) * 2 + c % 2


def pairs(target):
    return [
        (index(x, z, c), index(*target(x, z, c)))
        for x in range(2)
        for z in range(8)
        for c in range(2)
    ]


AHEAD = pairs(lambda x, z, c: (x, z + 1 - 2 * c, c))
BACK = pairs(lambda x, z, c: (x, z - 1 + 2 * c, c))
SIBLING = pairs(lambda x, z, c: (x, z, c + 1))
ACROSS = pairs(lambda x, z, c: (x + 1, z, c))
DIAGONAL = pairs(lambda x, z, c: (x + 1, z, c + 1))
PEERS = (SIBLING, ACROSS, DIAGONAL)

VMEM = pl.BlockSpec(memory_space=pltpu.VMEM)
SMEM = pl.BlockSpec(memory_space=pltpu.SMEM)
ANY = pl.BlockSpec(memory_space=pl.ANY)


def send(piece, table):
    return lax.ppermute(piece, "blk", table)


def column(start, size):
    return pl.ds(pl.multiple_of(start * size, size), size)


def pack_pool(head_ref, k_ref, v_ref, *outs):
    for j in range(PLANE):
        head = head_ref[j]
        outs[j][:, :DH] = k_ref[:, column(head, DH)]
        outs[j][:, DH:] = v_ref[:, column(head, DH)]


def pack_request(head_ref, q_ref, k_ref, v_ref, meta_ref, *outs):
    for j in range(PLANE):
        head = head_ref[j]
        outs[j][:, :GW] = q_ref[:, column(head, GW)]
        outs[j][:, GW : GW + DH] = k_ref[:, column(head, DH)]
        outs[j][:, GW + DH : GW + 2 * DH] = v_ref[:, column(head, DH)]
        outs[j][:, GW + 2 * DH :] = meta_ref[...]


def assemble(cuts, head_ref, *refs):
    total = sum(cuts)
    parts, out_ref, sems = refs[:total], refs[total], refs[total + 1]
    copies = []
    for j in range(PLANE):
        rows = BS // cuts[j]
        for i in range(cuts[j]):
            target = out_ref.at[i * rows : (i + 1) * rows, column(head_ref[j], GW)]
            at = len(copies)
            copies.append(pltpu.make_async_copy(parts[at].at[:rows], target, sems.at[at]))
    for copy in copies:
        copy.start()
    for copy in copies:
        copy.wait()


def attend(cuts, slot_ref, length_ref, *refs):
    n, total = len(cuts), sum(cuts)
    msgs, pieces, outs = refs[:n], refs[n : n + PIECES], refs[n + PIECES : n + PIECES + total]
    kv_ref, qs_ref, s_ref, own_ref, top_ref, acc_ref, sems = refs[n + PIECES + total :]
    copies = [
        pltpu.make_async_copy(pieces[i], kv_ref.at[pl.ds(i * HALF, HALF)], sems.at[i])
        for i in range(PIECES)
    ]
    for copy in copies:
        copy.start()
    row = lax.broadcasted_iota(jnp.int32, (ROWS, BS), 0) % BS
    causal = lax.broadcasted_iota(jnp.int32, (ROWS, BS), 1) <= row
    ones = jnp.ones((BS, DH), jnp.bfloat16)
    count = [(length_ref[r] + CHUNK - 1) // CHUNK for r in range(n)]

    def scores(r, keys):
        return (
            lax.dot_general(
                qs_ref[r], keys, (((1,), (1,)), ((), ())), preferred_element_type=jnp.float32
            )
            * SCALE
        )

    def own_scores(r):
        for h in range(G):
            qs_ref[r, h * BS : (h + 1) * BS, :] = msgs[r][:, h * DH : (h + 1) * DH]
        s = jnp.where(causal, scores(r, msgs[r][:, GW : GW + DH]), -jnp.inf)
        own_ref[r] = s
        top_ref[r] = s

    def entry(r, k, j):
        at = k * CHUNK + j
        live = at < length_ref[r]
        return slot_ref[r, jnp.where(live, at, 0)], live

    def chunk_scores(r, k):
        keys = jnp.concatenate([kv_ref[entry(r, k, j)[0], :, :DH] for j in range(CHUNK)], axis=0)
        s = scores(r, keys)
        s_ref[r, k] = s
        top = top_ref[r]
        for j in range(CHUNK):
            top = jnp.maximum(top, s[:, j * BS : (j + 1) * BS])
        top_ref[r] = top

    def own_values(r):
        top = jnp.broadcast_to(jnp.max(top_ref[r], axis=1, keepdims=True), (ROWS, BS))
        top_ref[r] = top
        w = jnp.exp2(own_ref[r] - top).astype(jnp.bfloat16)
        rhs = jnp.concatenate([msgs[r][:, GW + DH : GW + 2 * DH], ones], axis=1)
        acc_ref[...] = jnp.dot(w, rhs, preferred_element_type=jnp.float32)

    def chunk_values(r, k):
        w = jnp.exp2(s_ref[r, k] - jnp.tile(top_ref[r], (1, CHUNK))).astype(jnp.bfloat16)
        rhs = []
        for j in range(CHUNK):
            slot, live = entry(r, k, j)
            both = jnp.concatenate([kv_ref[slot, :, DH:], ones], axis=1)
            rhs.append(jnp.where(live, both, jnp.zeros_like(both)))
        acc_ref[...] += jnp.dot(w, jnp.concatenate(rhs, axis=0), preferred_element_type=jnp.float32)

    def finish(r):
        for h in range(G):
            a = acc_ref[h * BS : (h + 1) * BS, :]
            a = (a[:, :DH] / a[:, DH:]).astype(jnp.bfloat16)
            rows = BS // cuts[r]
            for i in range(cuts[r]):
                outs[sum(cuts[:r]) + i][:rows, h * DH : (h + 1) * DH] = a[i * rows : (i + 1) * rows]

    for out in outs:
        if out.shape[0] > BS:
            out[BS:] = jnp.zeros_like(out[BS:])
    own_scores(0)
    for copy in copies:
        copy.wait()

    @pl.loop(0, count[0])
    def _(k):
        chunk_scores(0, k)

    for r in range(n):
        own_values(r)
        if r + 1 < n:
            own_scores(r + 1)
            both = jnp.minimum(count[r], count[r + 1])

            @pl.loop(0, both)
            def _(k, r=r):
                chunk_values(r, k)
                chunk_scores(r + 1, k)

            @pl.loop(both, count[r])
            def _(k, r=r):
                chunk_values(r, k)

            @pl.loop(both, count[r + 1])
            def _(k, r=r):
                chunk_scores(r + 1, k)
        else:

            @pl.loop(0, count[r])
            def _(k, r=r):
                chunk_values(r, k)

        finish(r)


def run_attend(slots, lengths, msgs, pieces, cuts, extra=0):
    n = len(msgs)
    parts = [jax.ShapeDtypeStruct((BS // cut + extra, GW), jnp.bfloat16) for cut in cuts for _ in range(cut)]
    return pl.pallas_call(
        functools.partial(attend, cuts),
        out_shape=parts,
        in_specs=[SMEM] * 2 + [VMEM] * n + [ANY] * PIECES,
        out_specs=[VMEM] * len(parts),
        scratch_shapes=[
            pltpu.VMEM((PLANE * DEPTH, BS, 2 * DH), jnp.bfloat16),
            pltpu.VMEM((n, ROWS, DH), jnp.bfloat16),
            pltpu.VMEM((n, CHUNKS, ROWS, CHUNK * BS), jnp.float32),
            pltpu.VMEM((n, ROWS, BS), jnp.float32),
            pltpu.VMEM((n, ROWS, BS), jnp.float32),
            pltpu.VMEM((ROWS, 2 * DH), jnp.float32),
            pltpu.SemaphoreType.DMA((PIECES,)),
        ],
        cost_estimate=pl.CostEstimate(flops=1, bytes_accessed=1, transcendentals=1),
        compiler_params=pltpu.CompilerParams(vmem_limit_bytes=(12 + 12 * n) << 20),
    )(slots, lengths, *msgs, *pieces)


def body(queries, new_keys, new_values, prefix_keys, prefix_values, block_table, prefix_blocks):
    me = lax.axis_index("blk")
    x, z, c = me // 16, (me // 2) % 8, me % 2
    heads = jnp.stack([2 * x + c, 2 * x + 1 - c, 2 * (1 - x) + c, 2 * (1 - x) + 1 - c]).astype(jnp.int32)

    shard = jax.ShapeDtypeStruct((BS, 2 * DH), jnp.bfloat16)
    own, *outgoing = pl.pallas_call(
        pack_pool, out_shape=(shard,) * PLANE, in_specs=[SMEM, VMEM, VMEM], out_specs=(VMEM,) * PLANE,
        compiler_params=pltpu.CompilerParams(vmem_limit_bytes=8 << 20),
    )(heads, prefix_keys, prefix_values)
    arrived = [own] + [send(o, t) for o, t in zip(outgoing, PEERS)]
    first, second = jnp.stack(arrived[:HALF]), jnp.stack(arrived[HALF:])

    meta = jnp.concatenate([block_table[0], prefix_blocks]).astype(jnp.bfloat16)
    meta = jnp.broadcast_to(jnp.pad(meta, (0, DH - MAXB - 1))[None], (BS, DH))
    shard = jax.ShapeDtypeStruct((BS, MSG), jnp.bfloat16)
    own, *outgoing = pl.pallas_call(
        pack_request, out_shape=(shard,) * PLANE, in_specs=[SMEM] + [VMEM] * 4, out_specs=(VMEM,) * PLANE,
        compiler_params=pltpu.CompilerParams(vmem_limit_bytes=8 << 20),
    )(heads, queries, new_keys, new_values, meta)
    msgs = [own] + [send(o, t) for o, t in zip(outgoing, PEERS)]

    a, b = [(first, second)], [(first, second)]
    for step in range(4):
        a.append(tuple(send(p, AHEAD) for p in a[-1]))
        if step < 3:
            b.append(tuple(send(p, BACK) for p in b[-1]))
    pieces = [p for both in b + a[:0:-1] for p in both]
    msgs, pieces = lax.optimization_barrier((msgs, pieces))

    info = jnp.stack([m[0, GW + 2 * DH : GW + 2 * DH + MAXB + 1] for m in msgs]).astype(jnp.int32)
    table, lengths = info[:, :MAXB], info[:, MAXB]
    deep = (((table // 2) % 8 - z) * (1 - 2 * c)) % 8
    slots = deep * 4 + (table // 16 ^ x) * 2 + (table % 2 ^ c)

    across = run_attend(slots[2:3], lengths[2:3], msgs[2:3], pieces, (1,), extra=16)
    late, _ = lax.optimization_barrier((msgs[3], across))
    diagonal = run_attend(slots[3:], lengths[3:], [late], pieces, (1,))
    late, _ = lax.optimization_barrier((msgs[1], diagonal))
    *sibling, mine = run_attend(slots[1::-1], lengths[1::-1], [late, msgs[0]], pieces, (2, 1))
    parts = [
        [mine],
        [send(p, SIBLING) for p in sibling],
        [send(p, ACROSS) for p in across],
        [send(p, DIAGONAL) for p in diagonal],
    ]
    cuts = tuple(len(p) for p in parts)
    return pl.pallas_call(
        functools.partial(assemble, cuts),
        out_shape=jax.ShapeDtypeStruct(queries.shape, jnp.bfloat16),
        in_specs=[SMEM] + [VMEM] * sum(cuts),
        out_specs=ANY,
        scratch_shapes=[pltpu.SemaphoreType.DMA((sum(cuts),))],
        compiler_params=pltpu.CompilerParams(vmem_limit_bytes=8 << 20),
    )(heads, *[p for group in parts for p in group])


def solution(mesh):
    spec = P(("grp", "blk"), None)
    return jax.shard_map(
        body, mesh=mesh, in_specs=(spec,) * 6 + (P(("grp", "blk")),), out_specs=spec, check_vma=False
    )
```

```python
import functools
import math

import jax
import jax.numpy as jnp
from jax import lax
from jax.experimental import pallas as pl
from jax.experimental.pallas import tpu as pltpu
from jax.sharding import PartitionSpec as P

KVH = 4
DH = 128
BS = 128
G = 8
GW = G * DH
ROWS = G * BS
CHUNK = 4
MAXB = 16
CHUNKS = MAXB // CHUNK
MSG = GW + 3 * DH
PLANE = 4
DEPTH = 8
PIECES = 2 * DEPTH
HALF = PLANE // 2
SCALE = DH**-0.5 * math.log2(math.e)


def index(x, z, c):
    return ((x % 2) * 8 + z % 8) * 2 + c % 2


def pairs(target):
    return [
        (index(x, z, c), index(*target(x, z, c)))
        for x in range(2)
        for z in range(8)
        for c in range(2)
    ]


AHEAD = pairs(lambda x, z, c: (x, z + 1 - 2 * c, c))
BACK = pairs(lambda x, z, c: (x, z - 1 + 2 * c, c))
SIBLING = pairs(lambda x, z, c: (x, z, c + 1))
ACROSS = pairs(lambda x, z, c: (x + 1, z, c))
DIAGONAL = pairs(lambda x, z, c: (x + 1, z, c + 1))
PEERS = (SIBLING, ACROSS, DIAGONAL)

VMEM = pl.BlockSpec(memory_space=pltpu.VMEM)
SMEM = pl.BlockSpec(memory_space=pltpu.SMEM)
ANY = pl.BlockSpec(memory_space=pl.ANY)


def send(piece, table):
    return lax.ppermute(piece, "blk", table)


def column(start, size):
    return pl.ds(pl.multiple_of(start * size, size), size)


def pack(head_ref, pk_ref, pv_ref, q_ref, k_ref, v_ref, meta_ref, *outs):
    pool, request = outs[:PLANE], outs[PLANE:]
    for j in range(PLANE):
        head = head_ref[j]
        pool[j][:, :DH] = pk_ref[:, column(head, DH)]
        pool[j][:, DH:] = pv_ref[:, column(head, DH)]
    for j in range(PLANE):
        head = head_ref[j]
        request[j][:, :GW] = q_ref[:, column(head, GW)]
        request[j][:, GW : GW + DH] = k_ref[:, column(head, DH)]
        request[j][:, GW + DH : GW + 2 * DH] = v_ref[:, column(head, DH)]
        request[j][:, GW + 2 * DH :] = jnp.broadcast_to(meta_ref[...], (BS, DH))


def assemble(cuts, head_ref, *refs):
    total = sum(cuts)
    parts, out_ref, sems = refs[:total], refs[total], refs[total + 1]
    copies = []
    for j in range(PLANE):
        rows = BS // cuts[j]
        for i in range(cuts[j]):
            target = out_ref.at[i * rows : (i + 1) * rows, column(head_ref[j], GW)]
            at = len(copies)
            copies.append(pltpu.make_async_copy(parts[at], target, sems.at[at]))
    for copy in copies:
        copy.start()
    for copy in copies:
        copy.wait()


def attend(low, high, fresh, cuts, slot_ref, length_ref, *refs):
    n = 2
    count_pieces = (high - low) * 2
    refs = list(refs)

    def take(k):
        got = refs[:k]
        del refs[:k]
        return got

    msgs, pieces = take(n), take(count_pieces)
    state = [] if fresh else take(2)
    outs = take(sum(cuts) if cuts else 2)
    kv_ref, list_ref, qs_ref, s_ref, own_ref, top_ref, acc_ref, sems = refs
    copies = [
        pltpu.make_async_copy(pieces[i], kv_ref.at[pl.ds(i * HALF, HALF)], sems.at[i])
        for i in range(count_pieces)
    ]
    for copy in copies:
        copy.start()
    row = lax.broadcasted_iota(jnp.int32, (ROWS, BS), 0) % BS
    causal = lax.broadcasted_iota(jnp.int32, (ROWS, BS), 1) <= row
    ones = jnp.ones((BS, DH), jnp.bfloat16)

    sizes = []
    for r in range(n):

        def pick(i, size, r=r):
            slot = slot_ref[r, i] - low * PLANE
            inside = (slot >= 0) & (slot < (high - low) * PLANE)

            @pl.when(inside)
            def _():
                list_ref[r, size] = slot

            return size + inside.astype(jnp.int32)

        sizes.append(lax.fori_loop(0, length_ref[r], pick, 0))
    count = [(size + CHUNK - 1) // CHUNK for size in sizes]

    def scores(r, keys):
        return (
            lax.dot_general(
                qs_ref[r], keys, (((1,), (1,)), ((), ())), preferred_element_type=jnp.float32
            )
            * SCALE
        )

    def begin(r):
        for h in range(G):
            qs_ref[r, h * BS : (h + 1) * BS, :] = msgs[r][:, h * DH : (h + 1) * DH]
        if fresh:
            s = jnp.where(causal, scores(r, msgs[r][:, GW : GW + DH]), -jnp.inf)
            own_ref[r] = s
            top_ref[r] = s
        else:
            top_ref[r] = state[0][r]

    def entry(r, k, j):
        at = k * CHUNK + j
        live = at < sizes[r]
        return list_ref[r, jnp.where(live, at, 0)], live

    def chunk_scores(r, k):
        keys = jnp.concatenate([kv_ref[entry(r, k, j)[0], :, :DH] for j in range(CHUNK)], axis=0)
        s = scores(r, keys)
        s_ref[r, k] = s
        top = top_ref[r]
        for j in range(CHUNK):
            top = jnp.maximum(top, s[:, j * BS : (j + 1) * BS])
        top_ref[r] = top

    def turn(r):
        top = jnp.broadcast_to(jnp.max(top_ref[r], axis=1, keepdims=True), (ROWS, BS))
        top_ref[r] = top
        if fresh:
            w = jnp.exp2(own_ref[r] - top).astype(jnp.bfloat16)
            rhs = jnp.concatenate([msgs[r][:, GW + DH : GW + 2 * DH], ones], axis=1)
            acc_ref[...] = jnp.dot(w, rhs, preferred_element_type=jnp.float32)
        else:
            acc_ref[...] = state[1][r] * jnp.tile(jnp.exp2(state[0][r] - top), (1, 2))

    def chunk_values(r, k):
        w = jnp.exp2(s_ref[r, k] - jnp.tile(top_ref[r], (1, CHUNK))).astype(jnp.bfloat16)
        rhs = []
        for j in range(CHUNK):
            slot, live = entry(r, k, j)
            both = jnp.concatenate([kv_ref[slot, :, DH:], ones], axis=1)
            rhs.append(jnp.where(live, both, jnp.zeros_like(both)))
        acc_ref[...] += jnp.dot(w, jnp.concatenate(rhs, axis=0), preferred_element_type=jnp.float32)

    def finish(r):
        if not cuts:
            outs[0][r] = top_ref[r]
            outs[1][r] = acc_ref[...]
            return
        rows = BS // cuts[r]
        for h in range(G):
            a = acc_ref[h * BS : (h + 1) * BS, :]
            a = (a[:, :DH] / a[:, DH:]).astype(jnp.bfloat16)
            for i in range(cuts[r]):
                outs[sum(cuts[:r]) + i][:, h * DH : (h + 1) * DH] = a[i * rows : (i + 1) * rows]

    begin(0)
    for copy in copies:
        copy.wait()

    @pl.loop(0, count[0])
    def _(k):
        chunk_scores(0, k)

    turn(0)
    begin(1)
    both = jnp.minimum(count[0], count[1])

    @pl.loop(0, both)
    def _(k):
        chunk_values(0, k)
        chunk_scores(1, k)

    @pl.loop(both, count[0])
    def _(k):
        chunk_values(0, k)

    @pl.loop(both, count[1])
    def _(k):
        chunk_scores(1, k)

    finish(0)
    turn(1)

    @pl.loop(0, count[1])
    def _(k):
        chunk_values(1, k)

    finish(1)


def run_attend(slots, lengths, msgs, planes, low, high, state=(), cuts=()):
    n = len(msgs)
    pieces = [p for plane in planes[low:high] for p in plane]
    chunks = min(CHUNKS, high - low)
    if cuts:
        outs = [jax.ShapeDtypeStruct((BS // cut, GW), jnp.bfloat16) for cut in cuts for _ in range(cut)]
    else:
        outs = [jax.ShapeDtypeStruct((n, ROWS, w), jnp.float32) for w in (DH, 2 * DH)]
    return pl.pallas_call(
        functools.partial(attend, low, high, not state, cuts),
        out_shape=outs,
        in_specs=[SMEM] * 2 + [VMEM] * n + [ANY] * len(pieces) + [VMEM] * len(state),
        out_specs=[VMEM] * len(outs),
        scratch_shapes=[
            pltpu.VMEM((PLANE * (high - low), BS, 2 * DH), jnp.bfloat16),
            pltpu.SMEM((n, MAXB), jnp.int32),
            pltpu.VMEM((n, ROWS, DH), jnp.bfloat16),
            pltpu.VMEM((n, chunks, ROWS, CHUNK * BS), jnp.float32),
            pltpu.VMEM((n, ROWS, BS), jnp.float32),
            pltpu.VMEM((n, ROWS, BS), jnp.float32),
            pltpu.VMEM((ROWS, 2 * DH), jnp.float32),
            pltpu.SemaphoreType.DMA((len(pieces),)),
        ],
        cost_estimate=pl.CostEstimate(flops=1, bytes_accessed=1, transcendentals=1),
        compiler_params=pltpu.CompilerParams(vmem_limit_bytes=(20 + 4 * chunks) << 20),
    )(slots, lengths, *msgs, *pieces, *state)


def body(queries, new_keys, new_values, prefix_keys, prefix_values, block_table, prefix_blocks):
    me = lax.axis_index("blk")
    x, z, c = me // 16, (me // 2) % 8, me % 2
    heads = jnp.stack([2 * x + c, 2 * x + 1 - c, 2 * (1 - x) + c, 2 * (1 - x) + 1 - c]).astype(jnp.int32)

    meta = jnp.concatenate([block_table[0], prefix_blocks]).astype(jnp.bfloat16)
    meta = jnp.pad(meta, (0, DH - MAXB - 1))[None]
    shards = [jax.ShapeDtypeStruct((BS, w), jnp.bfloat16) for w in (2 * DH, MSG) for _ in range(PLANE)]
    packed = pl.pallas_call(
        pack,
        out_shape=shards,
        in_specs=[SMEM] + [VMEM] * 6,
        out_specs=[VMEM] * len(shards),
        compiler_params=pltpu.CompilerParams(vmem_limit_bytes=8 << 20),
    )(heads, prefix_keys, prefix_values, queries, new_keys, new_values, meta)
    pool, request = packed[:PLANE], packed[PLANE:]
    arrived = [pool[0]] + [send(o, t) for o, t in zip(pool[1:], PEERS)]
    first, second = jnp.stack(arrived[:HALF]), jnp.stack(arrived[HALF:])
    msgs = [request[0]] + [send(o, t) for o, t in zip(request[1:], PEERS)]

    a, b = [(first, second)], [(first, second)]
    for step in range(4):
        a.append(tuple(send(p, AHEAD) for p in a[-1]))
        if step < 3:
            b.append(tuple(send(p, BACK) for p in b[-1]))
    planes = [a[0], b[1], a[1], b[2], a[2], b[3], a[3], a[4]]

    info = jnp.stack([m[0, GW + 2 * DH : GW + 2 * DH + MAXB + 1] for m in msgs]).astype(jnp.int32)
    table, lengths = info[:, :MAXB], info[:, MAXB]
    deep = (((table // 2) % 8 - z) * (1 - 2 * c)) % 8
    order = jnp.where(deep < 4, jnp.maximum(2 * deep - 1, 0), jnp.minimum(2 * (8 - deep), 7))
    slots = order * 4 + (table // 16 ^ x) * 2 + (table % 2 ^ c)

    state = run_attend(slots[2:], lengths[2:], msgs[2:], planes, 0, 7)
    across, diagonal = run_attend(slots[2:], lengths[2:], msgs[2:], planes, 7, 8, state, (1, 1))
    late, _ = lax.optimization_barrier((msgs[1], diagonal))
    *sibling, mine = run_attend(slots[1::-1], lengths[1::-1], [late, msgs[0]], planes, 0, 8, (), (2, 1))
    parts = [
        [mine],
        [send(p, SIBLING) for p in sibling],
        [send(p, ACROSS) for p in [across]],
        [send(p, DIAGONAL) for p in [diagonal]],
    ]
    cuts = tuple(len(p) for p in parts)
    return pl.pallas_call(
        functools.partial(assemble, cuts),
        out_shape=jax.ShapeDtypeStruct(queries.shape, jnp.bfloat16),
        in_specs=[SMEM] + [VMEM] * sum(cuts),
        out_specs=ANY,
        scratch_shapes=[pltpu.SemaphoreType.DMA((sum(cuts),))],
        compiler_params=pltpu.CompilerParams(vmem_limit_bytes=8 << 20),
    )(heads, *[p for group in parts for p in group])


def solution(mesh):
    spec = P(("grp", "blk"), None)
    return jax.shard_map(
        body, mesh=mesh, in_specs=(spec,) * 6 + (P(("grp", "blk")),), out_specs=spec, check_vma=False
    )
```

```python
import functools
import math

import jax
import jax.numpy as jnp
from jax import lax
from jax.experimental import pallas as pl
from jax.experimental.pallas import tpu as pltpu
from jax.sharding import PartitionSpec as P

KVH = 4
DH = 128
BS = 128
G = 8
GW = G * DH
ROWS = G * BS
CHUNK = 4
MAXB = 16
CHUNKS = MAXB // CHUNK
MSG = GW + 3 * DH
PLANE = 4
DEPTH = 8
WAVE = 5
SCALE = DH**-0.5 * math.log2(math.e)


def index(x, z, c):
    return ((x % 2) * 8 + z % 8) * 2 + c % 2


def pairs(target):
    return [
        (index(x, z, c), index(*target(x, z, c)))
        for x in range(2)
        for z in range(8)
        for c in range(2)
    ]


AHEAD = pairs(lambda x, z, c: (x, z + 1 - 2 * c, c))
BACK = pairs(lambda x, z, c: (x, z - 1 + 2 * c, c))
SIBLING = pairs(lambda x, z, c: (x, z, c + 1))
ACROSS = pairs(lambda x, z, c: (x + 1, z, c))
DIAGONAL = pairs(lambda x, z, c: (x + 1, z, c + 1))
PEERS = (SIBLING, ACROSS, DIAGONAL)

VMEM = pl.BlockSpec(memory_space=pltpu.VMEM)
SMEM = pl.BlockSpec(memory_space=pltpu.SMEM)
ANY = pl.BlockSpec(memory_space=pl.ANY)
HBM = pl.BlockSpec(memory_space=pltpu.HBM)


def send(piece, table):
    return lax.ppermute(piece, "blk", table)


def column(start, size):
    return pl.ds(pl.multiple_of(start * size, size), size)


def peer_heads():
    me = lax.axis_index("blk")
    x, c = me // 16, me % 2
    return [2 * x + c, 2 * x + 1 - c, 2 * (1 - x) + c, 2 * (1 - x) + 1 - c]


def pack(table_ref, length_ref, pk_ref, pv_ref, q_ref, k_ref, v_ref, *refs):
    pool, request, sems = refs[:PLANE], refs[PLANE : 2 * PLANE], refs[2 * PLANE]
    copies = []

    def move(source, target):
        copies.append(pltpu.make_async_copy(source, target, sems.at[len(copies)]))
        copies[-1].start()

    heads = peer_heads()
    for j in range(PLANE):
        own = column(heads[j], DH)
        move(pk_ref.at[:, own], pool[j].at[:, :DH])
        move(pv_ref.at[:, own], pool[j].at[:, DH:])
    for j in range(PLANE):
        own = column(heads[j], DH)
        move(q_ref.at[:, column(heads[j], GW)], request[j].at[:, :GW])
        move(k_ref.at[:, own], request[j].at[:, GW : GW + DH])
        move(v_ref.at[:, own], request[j].at[:, GW + DH : GW + 2 * DH])
    lane = lax.broadcasted_iota(jnp.int32, (16, DH), 1)
    meta = jnp.where(lane == MAXB, length_ref[0], 0)
    for i in range(MAXB):
        meta = jnp.where(lane == i, table_ref[0, i], meta)
    meta = meta.astype(jnp.float32).astype(jnp.bfloat16)
    for j in range(PLANE):
        request[j][:16, GW + 2 * DH :] = meta
        request[j][16:, GW + 2 * DH :] = jnp.zeros((BS - 16, DH), jnp.bfloat16)
    for copy in copies:
        copy.wait()


def assemble(cuts, *refs):
    total = sum(cuts)
    heads = peer_heads()
    parts, out_ref, sems = refs[:total], refs[total], refs[total + 1]
    copies = []
    for j in range(PLANE):
        rows = BS // cuts[j]
        for i in range(cuts[j]):
            target = out_ref.at[i * rows : (i + 1) * rows, column(heads[j], GW)]
            at = len(copies)
            copies.append(pltpu.make_async_copy(parts[at], target, sems.at[at]))
    for copy in copies:
        copy.start()
    for copy in copies:
        copy.wait()


def attend(low, high, fresh, cuts, slot_ref, length_ref, *refs):
    n = 2
    count_pieces = high - low
    refs = list(refs)

    def take(k):
        got = refs[:k]
        del refs[:k]
        return got

    msgs, pieces = take(n), take(count_pieces)
    state = [] if fresh else take(2)
    outs = take(sum(cuts) if cuts else 2)
    kv_ref, list_ref, qs_ref, s_ref, own_ref, top_ref, acc_ref, sems = refs
    copies = [
        pltpu.make_async_copy(pieces[i], kv_ref.at[pl.ds(i * PLANE, PLANE)], sems.at[i])
        for i in range(count_pieces)
    ]
    for copy in copies:
        copy.start()
    row = lax.broadcasted_iota(jnp.int32, (ROWS, BS), 0) % BS
    causal = lax.broadcasted_iota(jnp.int32, (ROWS, BS), 1) <= row
    ones = jnp.ones((BS, DH), jnp.bfloat16)

    sizes = []
    for r in range(n):

        def pick(i, size, r=r):
            slot = slot_ref[r, i] - low * PLANE
            inside = (slot >= 0) & (slot < (high - low) * PLANE)

            @pl.when(inside)
            def _():
                list_ref[r, size] = slot

            return size + inside.astype(jnp.int32)

        sizes.append(lax.fori_loop(0, length_ref[r], pick, 0))
    count = [(size + CHUNK - 1) // CHUNK for size in sizes]

    def scores(r, keys):
        return (
            lax.dot_general(
                qs_ref[r], keys, (((1,), (1,)), ((), ())), preferred_element_type=jnp.float32
            )
            * SCALE
        )

    def begin(r):
        for h in range(G):
            qs_ref[r, h * BS : (h + 1) * BS, :] = msgs[r][:, h * DH : (h + 1) * DH]
        if fresh:
            s = jnp.where(causal, scores(r, msgs[r][:, GW : GW + DH]), -jnp.inf)
            own_ref[r] = s
            top_ref[r] = s
        else:
            top_ref[r] = state[0][r]

    def entry(r, k, j):
        at = k * CHUNK + j
        live = at < sizes[r]
        return list_ref[r, jnp.where(live, at, 0)], live

    def chunk_scores(r, k):
        keys = jnp.concatenate([kv_ref[entry(r, k, j)[0], :, :DH] for j in range(CHUNK)], axis=0)
        s = scores(r, keys)
        s_ref[r, k] = s
        top = top_ref[r]
        for j in range(CHUNK):
            top = jnp.maximum(top, s[:, j * BS : (j + 1) * BS])
        top_ref[r] = top

    def turn(r):
        top = jnp.broadcast_to(jnp.max(top_ref[r], axis=1, keepdims=True), (ROWS, BS))
        top_ref[r] = top
        if fresh:
            w = jnp.exp2(own_ref[r] - top).astype(jnp.bfloat16)
            rhs = jnp.concatenate([msgs[r][:, GW + DH : GW + 2 * DH], ones], axis=1)
            acc_ref[...] = jnp.dot(w, rhs, preferred_element_type=jnp.float32)
        else:
            acc_ref[...] = state[1][r] * jnp.tile(jnp.exp2(state[0][r] - top), (1, 2))

    def chunk_values(r, k):
        w = jnp.exp2(s_ref[r, k] - jnp.tile(top_ref[r], (1, CHUNK))).astype(jnp.bfloat16)
        rhs = []
        for j in range(CHUNK):
            slot, live = entry(r, k, j)
            both = jnp.concatenate([kv_ref[slot, :, DH:], ones], axis=1)
            rhs.append(jnp.where(live, both, jnp.zeros_like(both)))
        acc_ref[...] += jnp.dot(w, jnp.concatenate(rhs, axis=0), preferred_element_type=jnp.float32)

    def finish(r):
        if not cuts:
            outs[0][r] = top_ref[r]
            outs[1][r] = acc_ref[...]
            return
        rows = BS // cuts[r]
        for h in range(G):
            a = acc_ref[h * BS : (h + 1) * BS, :]
            a = (a[:, :DH] / a[:, DH:]).astype(jnp.bfloat16)
            for i in range(cuts[r]):
                outs[sum(cuts[:r]) + i][:, h * DH : (h + 1) * DH] = a[i * rows : (i + 1) * rows]

    begin(0)
    for copy in copies:
        copy.wait()

    @pl.loop(0, count[0])
    def _(k):
        chunk_scores(0, k)

    turn(0)
    begin(1)
    both = jnp.minimum(count[0], count[1])

    @pl.loop(0, both)
    def _(k):
        chunk_values(0, k)
        chunk_scores(1, k)

    @pl.loop(both, count[0])
    def _(k):
        chunk_values(0, k)

    @pl.loop(both, count[1])
    def _(k):
        chunk_scores(1, k)

    finish(0)
    turn(1)

    @pl.loop(0, count[1])
    def _(k):
        chunk_values(1, k)

    finish(1)


def run_attend(slots, lengths, msgs, planes, low, high, state=(), cuts=()):
    n = len(msgs)
    pieces = planes[low:high]
    chunks = min(CHUNKS, high - low)
    if cuts:
        outs = [jax.ShapeDtypeStruct((BS // cut, GW), jnp.bfloat16) for cut in cuts for _ in range(cut)]
    else:
        outs = [jax.ShapeDtypeStruct((n, ROWS, w), jnp.float32) for w in (DH, 2 * DH)]
    return pl.pallas_call(
        functools.partial(attend, low, high, not state, cuts),
        out_shape=outs,
        in_specs=[SMEM] * 2 + [VMEM] * n + [ANY] * len(pieces) + [VMEM] * len(state),
        out_specs=[VMEM] * len(outs),
        scratch_shapes=[
            pltpu.VMEM((PLANE * (high - low), BS, 2 * DH), jnp.bfloat16),
            pltpu.SMEM((n, MAXB), jnp.int32),
            pltpu.VMEM((n, ROWS, DH), jnp.bfloat16),
            pltpu.VMEM((n, chunks, ROWS, CHUNK * BS), jnp.float32),
            pltpu.VMEM((n, ROWS, BS), jnp.float32),
            pltpu.VMEM((n, ROWS, BS), jnp.float32),
            pltpu.VMEM((ROWS, 2 * DH), jnp.float32),
            pltpu.SemaphoreType.DMA((len(pieces),)),
        ],
        cost_estimate=pl.CostEstimate(flops=1, bytes_accessed=1, transcendentals=1),
        compiler_params=pltpu.CompilerParams(vmem_limit_bytes=(20 + 4 * chunks) << 20),
    )(slots, lengths, *msgs, *pieces, *state)


def body(queries, new_keys, new_values, prefix_keys, prefix_values, block_table, prefix_blocks):
    me = lax.axis_index("blk")
    x, z, c = me // 16, (me // 2) % 8, me % 2
    shards = [jax.ShapeDtypeStruct((BS, w), jnp.bfloat16) for w in (2 * DH, MSG) for _ in range(PLANE)]
    packed = pl.pallas_call(
        pack,
        out_shape=shards,
        in_specs=[SMEM] * 2 + [HBM] * 5,
        out_specs=[VMEM] * len(shards),
        scratch_shapes=[pltpu.SemaphoreType.DMA((5 * PLANE,))],
        compiler_params=pltpu.CompilerParams(vmem_limit_bytes=8 << 20),
    )(block_table, prefix_blocks, prefix_keys, prefix_values, queries, new_keys, new_values)
    pool, request = packed[:PLANE], packed[PLANE:]
    arrived = [pool[0]] + [send(o, t) for o, t in zip(pool[1:], PEERS)]
    piece = jnp.stack(arrived)
    msgs = [request[0]] + [send(o, t) for o, t in zip(request[1:], PEERS)]

    a, b = [piece], [piece]
    for _ in range(3):
        a.append(send(a[-1], AHEAD))
        b.append(send(b[-1], BACK))
    planes = [a[0], b[1], a[1], b[2], a[2], b[3], a[3]]

    info = jnp.stack([m[0, GW + 2 * DH : GW + 2 * DH + MAXB + 1] for m in msgs]).astype(jnp.int32)
    table, lengths = info[:, :MAXB], info[:, MAXB]
    deep = (((table // 2) % 8 - z) * (1 - 2 * c)) % 8
    order = jnp.where(deep < 4, jnp.maximum(2 * deep - 1, 0), jnp.minimum(2 * (8 - deep), 7))
    slots = order * 4 + (table // 16 ^ x) * 2 + (table % 2 ^ c)

    state = run_attend(slots[2:], lengths[2:], msgs[2:], planes, 0, WAVE)
    last, state = lax.optimization_barrier((a[3], state))
    planes.append(send(last, AHEAD))
    across, diagonal = run_attend(slots[2:], lengths[2:], msgs[2:], planes, WAVE, DEPTH, state, (1, 1))
    late, _ = lax.optimization_barrier((msgs[1], diagonal))
    *sibling, mine = run_attend(slots[1::-1], lengths[1::-1], [late, msgs[0]], planes, 0, DEPTH, (), (2, 1))
    parts = [
        [mine],
        [send(p, SIBLING) for p in sibling],
        [send(p, ACROSS) for p in [across]],
        [send(p, DIAGONAL) for p in [diagonal]],
    ]
    cuts = tuple(len(p) for p in parts)
    return pl.pallas_call(
        functools.partial(assemble, cuts),
        out_shape=jax.ShapeDtypeStruct(queries.shape, jnp.bfloat16),
        in_specs=[VMEM] * sum(cuts),
        out_specs=ANY,
        scratch_shapes=[pltpu.SemaphoreType.DMA((sum(cuts),))],
        compiler_params=pltpu.CompilerParams(vmem_limit_bytes=8 << 20),
    )(*[p for group in parts for p in group])


def solution(mesh):
    spec = P(("grp", "blk"), None)
    return jax.shard_map(
        body, mesh=mesh, in_specs=(spec,) * 6 + (P(("grp", "blk")),), out_specs=spec, check_vma=False
    )
```

```python
import functools
import math

import jax
import jax.numpy as jnp
from jax import lax
from jax.experimental import pallas as pl
from jax.experimental.pallas import tpu as pltpu
from jax.sharding import PartitionSpec as P

KVH = 4
DH = 128
BS = 128
G = 8
GW = G * DH
ROWS = G * BS
CHUNK = 4
MAXB = 16
CHUNKS = MAXB // CHUNK
MSG = GW + 3 * DH
PLANE = 4
DEPTH = 8
WAVE = 5
SCALE = DH**-0.5 * math.log2(math.e)


def index(x, z, c):
    return ((x % 2) * 8 + z % 8) * 2 + c % 2


def pairs(target):
    return [
        (index(x, z, c), index(*target(x, z, c)))
        for x in range(2)
        for z in range(8)
        for c in range(2)
    ]


AHEAD = pairs(lambda x, z, c: (x, z + 1 - 2 * c, c))
BACK = pairs(lambda x, z, c: (x, z - 1 + 2 * c, c))
SIBLING = pairs(lambda x, z, c: (x, z, c + 1))
ACROSS = pairs(lambda x, z, c: (x + 1, z, c))
DIAGONAL = pairs(lambda x, z, c: (x + 1, z, c + 1))
PEERS = (SIBLING, ACROSS, DIAGONAL)

VMEM = pl.BlockSpec(memory_space=pltpu.VMEM)
SMEM = pl.BlockSpec(memory_space=pltpu.SMEM)
ANY = pl.BlockSpec(memory_space=pl.ANY)
HBM = pl.BlockSpec(memory_space=pltpu.HBM)


def send(piece, table):
    return lax.ppermute(piece, "blk", table)


def column(start, size):
    return pl.ds(pl.multiple_of(start * size, size), size)


def peer_heads():
    me = lax.axis_index("blk")
    x, c = me // 16, me % 2
    return [2 * x + c, 2 * x + 1 - c, 2 * (1 - x) + c, 2 * (1 - x) + 1 - c]


def pack(table_ref, length_ref, pk_ref, pv_ref, q_ref, k_ref, v_ref, *refs):
    pool, request, sems = refs[:PLANE], refs[PLANE : 2 * PLANE], refs[2 * PLANE]
    copies = []

    def move(source, target):
        copies.append(pltpu.make_async_copy(source, target, sems.at[len(copies)]))
        copies[-1].start()

    heads = peer_heads()
    for j in range(PLANE):
        own = column(heads[j], DH)
        move(pk_ref.at[:, own], pool[j].at[:, :DH])
        move(pv_ref.at[:, own], pool[j].at[:, DH:])
    for j in range(PLANE):
        own = column(heads[j], DH)
        move(q_ref.at[:, column(heads[j], GW)], request[j].at[:, :GW])
        move(k_ref.at[:, own], request[j].at[:, GW : GW + DH])
        move(v_ref.at[:, own], request[j].at[:, GW + DH : GW + 2 * DH])
    lane = lax.broadcasted_iota(jnp.int32, (16, DH), 1)
    meta = jnp.where(lane == MAXB, length_ref[0], 0)
    for i in range(MAXB):
        meta = jnp.where(lane == i, table_ref[0, i], meta)
    meta = meta.astype(jnp.float32).astype(jnp.bfloat16)
    for j in range(PLANE):
        request[j][:16, GW + 2 * DH :] = meta
        request[j][16:, GW + 2 * DH :] = jnp.zeros((BS - 16, DH), jnp.bfloat16)
    for copy in copies:
        copy.wait()


def assemble(cuts, *refs):
    total = sum(cuts)
    heads = peer_heads()
    parts, out_ref, sems = refs[:total], refs[total], refs[total + 1]
    copies = []
    for j in range(PLANE):
        rows = BS // cuts[j]
        for i in range(cuts[j]):
            target = out_ref.at[i * rows : (i + 1) * rows, column(heads[j], GW)]
            at = len(copies)
            copies.append(pltpu.make_async_copy(parts[at], target, sems.at[at]))
    for copy in copies:
        copy.start()
    for copy in copies:
        copy.wait()


def attend(low, high, fresh, cuts, slot_ref, length_ref, *refs):
    n = 2
    count_pieces = high - low
    refs = list(refs)

    def take(k):
        got = refs[:k]
        del refs[:k]
        return got

    msgs, pieces = take(n), take(count_pieces)
    state = [] if fresh else take(2)
    outs = take(sum(cuts) if cuts else 2)
    kv_ref, list_ref, qs_ref, s_ref, own_ref, top_ref, acc_ref, sems = refs
    copies = [
        pltpu.make_async_copy(pieces[i], kv_ref.at[pl.ds(i * PLANE, PLANE)], sems.at[i])
        for i in range(count_pieces)
    ]
    for copy in copies:
        copy.start()
    row = lax.broadcasted_iota(jnp.int32, (ROWS, BS), 0) % BS
    causal = lax.broadcasted_iota(jnp.int32, (ROWS, BS), 1) <= row
    ones = jnp.ones((BS, DH), jnp.bfloat16)

    sizes = []
    for r in range(n):

        def pick(i, size, r=r):
            slot = slot_ref[r, i] - low * PLANE
            inside = (slot >= 0) & (slot < (high - low) * PLANE)

            @pl.when(inside)
            def _():
                list_ref[r, size] = slot

            return size + inside.astype(jnp.int32)

        sizes.append(lax.fori_loop(0, length_ref[r], pick, 0))
    count = [(size + CHUNK - 1) // CHUNK for size in sizes]

    def scores(r, keys):
        return (
            lax.dot_general(
                qs_ref[r], keys, (((1,), (1,)), ((), ())), preferred_element_type=jnp.float32
            )
            * SCALE
        )

    def begin(r):
        for h in range(G):
            qs_ref[r, h * BS : (h + 1) * BS, :] = msgs[r][:, h * DH : (h + 1) * DH]
        if fresh:
            s = jnp.where(causal, scores(r, msgs[r][:, GW : GW + DH]), -jnp.inf)
            own_ref[r] = s
            top_ref[r] = s
        else:
            top_ref[r] = state[0][r]

    def entry(r, k, j):
        at = k * CHUNK + j
        live = at < sizes[r]
        return list_ref[r, jnp.where(live, at, 0)], live

    def chunk_scores(r, k):
        keys = jnp.concatenate([kv_ref[entry(r, k, j)[0], :, :DH] for j in range(CHUNK)], axis=0)
        s = scores(r, keys)
        s_ref[r, k] = s
        top = top_ref[r]
        for j in range(CHUNK):
            top = jnp.maximum(top, s[:, j * BS : (j + 1) * BS])
        top_ref[r] = top

    def turn(r):
        top = jnp.broadcast_to(jnp.max(top_ref[r], axis=1, keepdims=True), (ROWS, BS))
        top_ref[r] = top
        if fresh:
            w = jnp.exp2(own_ref[r] - top).astype(jnp.bfloat16)
            rhs = jnp.concatenate([msgs[r][:, GW + DH : GW + 2 * DH], ones], axis=1)
            acc_ref[...] = jnp.dot(w, rhs, preferred_element_type=jnp.float32)
        else:
            acc_ref[...] = state[1][r] * jnp.tile(jnp.exp2(state[0][r] - top), (1, 2))

    def chunk_values(r, k):
        w = jnp.exp2(s_ref[r, k] - jnp.tile(top_ref[r], (1, CHUNK))).astype(jnp.bfloat16)
        rhs = []
        for j in range(CHUNK):
            slot, live = entry(r, k, j)
            both = jnp.concatenate([kv_ref[slot, :, DH:], ones], axis=1)
            rhs.append(jnp.where(live, both, jnp.zeros_like(both)))
        acc_ref[...] += jnp.dot(w, jnp.concatenate(rhs, axis=0), preferred_element_type=jnp.float32)

    def finish(r):
        if not cuts:
            outs[0][r] = top_ref[r]
            outs[1][r] = acc_ref[...]
            return
        rows = BS // cuts[r]
        for h in range(G):
            a = acc_ref[h * BS : (h + 1) * BS, :]
            a = (a[:, :DH] / a[:, DH:]).astype(jnp.bfloat16)
            for i in range(cuts[r]):
                outs[sum(cuts[:r]) + i][:, h * DH : (h + 1) * DH] = a[i * rows : (i + 1) * rows]

    begin(0)
    for copy in copies:
        copy.wait()

    @pl.loop(0, count[0])
    def _(k):
        chunk_scores(0, k)

    turn(0)
    begin(1)
    both = jnp.minimum(count[0], count[1])

    @pl.loop(0, both)
    def _(k):
        chunk_values(0, k)
        chunk_scores(1, k)

    @pl.loop(both, count[0])
    def _(k):
        chunk_values(0, k)

    @pl.loop(both, count[1])
    def _(k):
        chunk_scores(1, k)

    finish(0)
    turn(1)

    @pl.loop(0, count[1])
    def _(k):
        chunk_values(1, k)

    finish(1)


def run_attend(slots, lengths, msgs, planes, low, high, state=(), cuts=()):
    n = len(msgs)
    pieces = planes[low:high]
    chunks = min(CHUNKS, high - low)
    if cuts:
        outs = [jax.ShapeDtypeStruct((BS // cut, GW), jnp.bfloat16) for cut in cuts for _ in range(cut)]
    else:
        outs = [jax.ShapeDtypeStruct((n, ROWS, w), jnp.float32) for w in (DH, 2 * DH)]
    return pl.pallas_call(
        functools.partial(attend, low, high, not state, cuts),
        out_shape=outs,
        in_specs=[SMEM] * 2 + [VMEM] * n + [ANY] * len(pieces) + [VMEM] * len(state),
        out_specs=[VMEM] * len(outs),
        scratch_shapes=[
            pltpu.VMEM((PLANE * (high - low), BS, 2 * DH), jnp.bfloat16),
            pltpu.SMEM((n, MAXB), jnp.int32),
            pltpu.VMEM((n, ROWS, DH), jnp.bfloat16),
            pltpu.VMEM((n, chunks, ROWS, CHUNK * BS), jnp.float32),
            pltpu.VMEM((n, ROWS, BS), jnp.float32),
            pltpu.VMEM((n, ROWS, BS), jnp.float32),
            pltpu.VMEM((ROWS, 2 * DH), jnp.float32),
            pltpu.SemaphoreType.DMA((len(pieces),)),
        ],
        cost_estimate=pl.CostEstimate(flops=1, bytes_accessed=1, transcendentals=1),
        compiler_params=pltpu.CompilerParams(vmem_limit_bytes=(20 + 4 * chunks) << 20),
    )(slots, lengths, *msgs, *pieces, *state)


def body(queries, new_keys, new_values, prefix_keys, prefix_values, block_table, prefix_blocks):
    me = lax.axis_index("blk")
    x, z, c = me // 16, (me // 2) % 8, me % 2
    shards = [jax.ShapeDtypeStruct((BS, w), jnp.bfloat16) for w in (2 * DH, MSG) for _ in range(PLANE)]
    packed = pl.pallas_call(
        pack,
        out_shape=shards,
        in_specs=[SMEM] * 2 + [HBM] * 5,
        out_specs=[VMEM] * len(shards),
        scratch_shapes=[pltpu.SemaphoreType.DMA((5 * PLANE,))],
    )(block_table, prefix_blocks, prefix_keys, prefix_values, queries, new_keys, new_values)
    pool, request = packed[:PLANE], packed[PLANE:]
    arrived = [pool[0]] + [send(o, t) for o, t in zip(pool[1:], PEERS)]
    piece = jnp.stack(arrived)
    msgs = [request[0]] + [send(o, t) for o, t in zip(request[1:], PEERS)]

    a, b = [piece], [piece]
    for _ in range(3):
        a.append(send(a[-1], AHEAD))
        b.append(send(b[-1], BACK))
    planes = [a[0], b[1], a[1], b[2], a[2], b[3], a[3]]

    info = jnp.stack([m[0, GW + 2 * DH : GW + 2 * DH + MAXB + 1] for m in msgs]).astype(jnp.int32)
    table, lengths = info[:, :MAXB], info[:, MAXB]
    deep = (((table // 2) % 8 - z) * (1 - 2 * c)) % 8
    order = jnp.where(deep < 4, jnp.maximum(2 * deep - 1, 0), jnp.minimum(2 * (8 - deep), 7))
    slots = order * 4 + (table // 16 ^ x) * 2 + (table % 2 ^ c)

    state = run_attend(slots[2:], lengths[2:], msgs[2:], planes, 0, WAVE)
    last, state = lax.optimization_barrier((a[3], state))
    planes.append(send(last, AHEAD))
    state = run_attend(slots[2:], lengths[2:], msgs[2:], planes, WAVE, DEPTH - 1, state)
    across, diagonal = run_attend(slots[2:], lengths[2:], msgs[2:], planes, DEPTH - 1, DEPTH, state, (1, 1))
    late, _ = lax.optimization_barrier((msgs[1], diagonal))
    *sibling, mine = run_attend(slots[1::-1], lengths[1::-1], [late, msgs[0]], planes, 0, DEPTH, (), (2, 1))
    parts = [
        [mine],
        [send(p, SIBLING) for p in sibling],
        [send(p, ACROSS) for p in [across]],
        [send(p, DIAGONAL) for p in [diagonal]],
    ]
    cuts = tuple(len(p) for p in parts)
    return pl.pallas_call(
        functools.partial(assemble, cuts),
        out_shape=jax.ShapeDtypeStruct(queries.shape, jnp.bfloat16),
        in_specs=[VMEM] * sum(cuts),
        out_specs=ANY,
        scratch_shapes=[pltpu.SemaphoreType.DMA((sum(cuts),))],
        compiler_params=pltpu.CompilerParams(vmem_limit_bytes=8 << 20),
    )(*[p for group in parts for p in group])


def solution(mesh):
    spec = P(("grp", "blk"), None)
    return jax.shard_map(
        body, mesh=mesh, in_specs=(spec,) * 6 + (P(("grp", "blk")),), out_specs=spec, check_vma=False
    )
```

```python
import functools
import math

import jax
import jax.numpy as jnp
from jax import lax
from jax.experimental import pallas as pl
from jax.experimental.pallas import tpu as pltpu
from jax.sharding import PartitionSpec as P

KVH = 4
DH = 128
BS = 128
G = 8
GW = G * DH
ROWS = G * BS
CHUNK = 4
MAXB = 16
CHUNKS = MAXB // CHUNK
MSG = GW + 3 * DH
PLANE = 4
DEPTH = 8
WAVE = 5
NEAR = 3
SCALE = DH**-0.5 * math.log2(math.e)


def index(x, z, c):
    return ((x % 2) * 8 + z % 8) * 2 + c % 2


def pairs(target):
    return [
        (index(x, z, c), index(*target(x, z, c)))
        for x in range(2)
        for z in range(8)
        for c in range(2)
    ]


AHEAD = pairs(lambda x, z, c: (x, z + 1 - 2 * c, c))
BACK = pairs(lambda x, z, c: (x, z - 1 + 2 * c, c))
SIBLING = pairs(lambda x, z, c: (x, z, c + 1))
ACROSS = pairs(lambda x, z, c: (x + 1, z, c))
DIAGONAL = pairs(lambda x, z, c: (x + 1, z, c + 1))
PEERS = (SIBLING, ACROSS, DIAGONAL)

VMEM = pl.BlockSpec(memory_space=pltpu.VMEM)
SMEM = pl.BlockSpec(memory_space=pltpu.SMEM)
ANY = pl.BlockSpec(memory_space=pl.ANY)
HBM = pl.BlockSpec(memory_space=pltpu.HBM)


def send(piece, table):
    return lax.ppermute(piece, "blk", table)


def column(start, size):
    return pl.ds(pl.multiple_of(start * size, size), size)


def peer_heads():
    me = lax.axis_index("blk")
    x, c = me // 16, me % 2
    return [2 * x + c, 2 * x + 1 - c, 2 * (1 - x) + c, 2 * (1 - x) + 1 - c]


def mover(copies, sems):
    def move(source, target):
        copies.append(pltpu.make_async_copy(source, target, sems.at[len(copies)]))
        copies[-1].start()

    return move


def pack_pool(k_ref, v_ref, *refs):
    outs, copies = refs[:PLANE], []
    move = mover(copies, refs[PLANE])
    heads = peer_heads()
    for j in (1, 2, 3, 0):
        own = column(heads[j], DH)
        move(k_ref.at[:, own], outs[j].at[:, :DH])
        move(v_ref.at[:, own], outs[j].at[:, DH:])
    for copy in copies:
        copy.wait()


def pack_request(table_ref, length_ref, q_ref, k_ref, v_ref, *refs):
    outs, copies = refs[:PLANE], []
    move = mover(copies, refs[PLANE])
    heads = peer_heads()
    for j in (2, 3, 1, 0):
        own = column(heads[j], DH)
        move(q_ref.at[:, column(heads[j], GW)], outs[j].at[:, :GW])
        move(k_ref.at[:, own], outs[j].at[:, GW : GW + DH])
        move(v_ref.at[:, own], outs[j].at[:, GW + DH : GW + 2 * DH])
    lane = lax.broadcasted_iota(jnp.int32, (16, DH), 1)
    meta = jnp.where(lane == MAXB, length_ref[0], 0)
    for i in range(MAXB):
        meta = jnp.where(lane == i, table_ref[0, i], meta)
    meta = meta.astype(jnp.float32).astype(jnp.bfloat16)
    for j in range(PLANE):
        outs[j][:16, GW + 2 * DH :] = meta
        outs[j][16:, GW + 2 * DH :] = jnp.zeros((BS - 16, DH), jnp.bfloat16)
    for copy in copies:
        copy.wait()


def assemble(cuts, *refs):
    total = sum(cuts)
    heads = peer_heads()
    parts, out_ref, sems = refs[:total], refs[total], refs[total + 1]
    copies = []
    for j in range(PLANE):
        rows = BS // cuts[j]
        for i in range(cuts[j]):
            target = out_ref.at[i * rows : (i + 1) * rows, column(heads[j], GW)]
            at = len(copies)
            copies.append(pltpu.make_async_copy(parts[at], target, sems.at[at]))
    for copy in copies:
        copy.start()
    for copy in copies:
        copy.wait()


def attend(low, high, fresh, cuts, slot_ref, length_ref, *refs):
    n = 2
    count_pieces = high - low
    refs = list(refs)

    def take(k):
        got = refs[:k]
        del refs[:k]
        return got

    msgs, pieces = take(n), take(count_pieces)
    state = [] if fresh else take(2)
    outs = take(sum(cuts) if cuts else 2)
    kv_ref, list_ref, qs_ref, s_ref, own_ref, top_ref, acc_ref, sems = refs
    copies = [
        pltpu.make_async_copy(pieces[i], kv_ref.at[pl.ds(i * PLANE, PLANE)], sems.at[i])
        for i in range(count_pieces)
    ]
    for copy in copies:
        copy.start()
    row = lax.broadcasted_iota(jnp.int32, (ROWS, BS), 0) % BS
    causal = lax.broadcasted_iota(jnp.int32, (ROWS, BS), 1) <= row
    ones = jnp.ones((BS, DH), jnp.bfloat16)

    sizes = []
    for r in range(n):

        def pick(i, size, r=r):
            slot = slot_ref[r, i] - low * PLANE
            inside = (slot >= 0) & (slot < (high - low) * PLANE)

            @pl.when(inside)
            def _():
                list_ref[r, size] = slot

            return size + inside.astype(jnp.int32)

        sizes.append(lax.fori_loop(0, length_ref[r], pick, 0))
    count = [(size + CHUNK - 1) // CHUNK for size in sizes]

    def scores(r, keys):
        return (
            lax.dot_general(
                qs_ref[r], keys, (((1,), (1,)), ((), ())), preferred_element_type=jnp.float32
            )
            * SCALE
        )

    def begin(r):
        for h in range(G):
            qs_ref[r, h * BS : (h + 1) * BS, :] = msgs[r][:, h * DH : (h + 1) * DH]
        if fresh:
            s = jnp.where(causal, scores(r, msgs[r][:, GW : GW + DH]), -jnp.inf)
            own_ref[r] = s
            top_ref[r] = s
        else:
            top_ref[r] = state[0][r]

    def entry(r, k, j):
        at = k * CHUNK + j
        live = at < sizes[r]
        return list_ref[r, jnp.where(live, at, 0)], live

    def chunk_scores(r, k):
        keys = jnp.concatenate([kv_ref[entry(r, k, j)[0], :, :DH] for j in range(CHUNK)], axis=0)
        s = scores(r, keys)
        s_ref[r, k] = s
        top = top_ref[r]
        for j in range(CHUNK):
            top = jnp.maximum(top, s[:, j * BS : (j + 1) * BS])
        top_ref[r] = top

    def turn(r):
        top = jnp.broadcast_to(jnp.max(top_ref[r], axis=1, keepdims=True), (ROWS, BS))
        top_ref[r] = top
        if fresh:
            w = jnp.exp2(own_ref[r] - top).astype(jnp.bfloat16)
            rhs = jnp.concatenate([msgs[r][:, GW + DH : GW + 2 * DH], ones], axis=1)
            acc_ref[...] = jnp.dot(w, rhs, preferred_element_type=jnp.float32)
        else:
            acc_ref[...] = state[1][r] * jnp.tile(jnp.exp2(state[0][r] - top), (1, 2))

    def chunk_values(r, k):
        w = jnp.exp2(s_ref[r, k] - jnp.tile(top_ref[r], (1, CHUNK))).astype(jnp.bfloat16)
        rhs = []
        for j in range(CHUNK):
            slot, live = entry(r, k, j)
            both = jnp.concatenate([kv_ref[slot, :, DH:], ones], axis=1)
            rhs.append(jnp.where(live, both, jnp.zeros_like(both)))
        acc_ref[...] += jnp.dot(w, jnp.concatenate(rhs, axis=0), preferred_element_type=jnp.float32)

    def finish(r):
        if not cuts:
            outs[0][r] = top_ref[r]
            outs[1][r] = acc_ref[...]
            return
        rows = BS // cuts[r]
        for h in range(G):
            a = acc_ref[h * BS : (h + 1) * BS, :]
            a = (a[:, :DH] / a[:, DH:]).astype(jnp.bfloat16)
            for i in range(cuts[r]):
                outs[sum(cuts[:r]) + i][:, h * DH : (h + 1) * DH] = a[i * rows : (i + 1) * rows]

    begin(0)
    for copy in copies:
        copy.wait()

    @pl.loop(0, count[0])
    def _(k):
        chunk_scores(0, k)

    turn(0)
    begin(1)
    both = jnp.minimum(count[0], count[1])

    @pl.loop(0, both)
    def _(k):
        chunk_values(0, k)
        chunk_scores(1, k)

    @pl.loop(both, count[0])
    def _(k):
        chunk_values(0, k)

    @pl.loop(both, count[1])
    def _(k):
        chunk_scores(1, k)

    finish(0)
    turn(1)

    @pl.loop(0, count[1])
    def _(k):
        chunk_values(1, k)

    finish(1)


def run_attend(slots, lengths, msgs, planes, low, high, state=(), cuts=()):
    n = len(msgs)
    pieces = planes[low:high]
    chunks = min(CHUNKS, high - low)
    if cuts:
        outs = [jax.ShapeDtypeStruct((BS // cut, GW), jnp.bfloat16) for cut in cuts for _ in range(cut)]
    else:
        outs = [jax.ShapeDtypeStruct((n, ROWS, w), jnp.float32) for w in (DH, 2 * DH)]
    return pl.pallas_call(
        functools.partial(attend, low, high, not state, cuts),
        out_shape=outs,
        in_specs=[SMEM] * 2 + [VMEM] * n + [ANY] * len(pieces) + [VMEM] * len(state),
        out_specs=[VMEM] * len(outs),
        scratch_shapes=[
            pltpu.VMEM((PLANE * (high - low), BS, 2 * DH), jnp.bfloat16),
            pltpu.SMEM((n, MAXB), jnp.int32),
            pltpu.VMEM((n, ROWS, DH), jnp.bfloat16),
            pltpu.VMEM((n, chunks, ROWS, CHUNK * BS), jnp.float32),
            pltpu.VMEM((n, ROWS, BS), jnp.float32),
            pltpu.VMEM((n, ROWS, BS), jnp.float32),
            pltpu.VMEM((ROWS, 2 * DH), jnp.float32),
            pltpu.SemaphoreType.DMA((len(pieces),)),
        ],
        cost_estimate=pl.CostEstimate(flops=1, bytes_accessed=1, transcendentals=1),
        compiler_params=pltpu.CompilerParams(vmem_limit_bytes=(20 + 4 * chunks) << 20),
    )(slots, lengths, *msgs, *pieces, *state)


def body(queries, new_keys, new_values, prefix_keys, prefix_values, block_table, prefix_blocks):
    pool = pl.pallas_call(
        pack_pool,
        out_shape=[jax.ShapeDtypeStruct((BS, 2 * DH), jnp.bfloat16)] * PLANE,
        in_specs=[HBM] * 2,
        out_specs=[VMEM] * PLANE,
        scratch_shapes=[pltpu.SemaphoreType.DMA((2 * PLANE,))],
    )(prefix_keys, prefix_values)
    ahead, _ = lax.optimization_barrier((queries, pool))
    request = pl.pallas_call(
        pack_request,
        out_shape=[jax.ShapeDtypeStruct((BS, MSG), jnp.bfloat16)] * PLANE,
        in_specs=[SMEM] * 2 + [HBM] * 3,
        out_specs=[VMEM] * PLANE,
        scratch_shapes=[pltpu.SemaphoreType.DMA((3 * PLANE,))],
        cost_estimate=pl.CostEstimate(flops=1, bytes_accessed=1, transcendentals=1),
    )(block_table, prefix_blocks, ahead, new_keys, new_values)
    arrived = [pool[0]] + [send(o, t) for o, t in zip(pool[1:], PEERS)]
    arrived, request = lax.optimization_barrier((arrived, request))
    piece = jnp.stack(arrived)
    msgs = [request[0]] + [send(o, t) for o, t in zip(request[1:], PEERS)]

    me = lax.axis_index("blk")
    x, z, c = me // 16, (me // 2) % 8, me % 2

    def entries(chosen):
        info = jnp.stack([m[0, GW + 2 * DH : GW + 2 * DH + MAXB + 1] for m in chosen]).astype(jnp.int32)
        table, lengths = info[:, :MAXB], info[:, MAXB]
        deep = (((table // 2) % 8 - z) * (1 - 2 * c)) % 8
        order = jnp.where(deep < 4, jnp.maximum(2 * deep - 1, 0), jnp.minimum(2 * (8 - deep), 7))
        return order * 4 + (table // 16 ^ x) * 2 + (table % 2 ^ c), lengths

    near, far = msgs[1::-1], msgs[2:]
    near_work, far_work = entries(near), entries(far)
    a, b = [piece], [piece]
    for _ in range(2):
        a.append(send(a[-1], AHEAD))
        b.append(send(b[-1], BACK))
    planes = [a[0], b[1], a[1], b[2], a[2]]
    near_state = run_attend(*near_work, near, planes, 0, NEAR)
    last, near_state = lax.optimization_barrier(((a[2], b[2]), near_state))
    planes += [send(last[1], BACK), send(last[0], AHEAD)]
    state = run_attend(*far_work, far, planes, 0, WAVE)
    last, state = lax.optimization_barrier((planes[-1], state))
    planes.append(send(last, AHEAD))
    state = run_attend(*far_work, far, planes, WAVE, DEPTH - 1, state)
    across, diagonal = run_attend(*far_work, far, planes, DEPTH - 1, DEPTH, state, (1, 1))
    near_state, _ = lax.optimization_barrier((near_state, diagonal))
    *sibling, mine = run_attend(*near_work, near, planes, NEAR, DEPTH, near_state, (2, 1))
    parts = [
        [mine],
        [send(p, SIBLING) for p in sibling],
        [send(p, ACROSS) for p in [across]],
        [send(p, DIAGONAL) for p in [diagonal]],
    ]
    cuts = tuple(len(p) for p in parts)
    return pl.pallas_call(
        functools.partial(assemble, cuts),
        out_shape=jax.ShapeDtypeStruct(queries.shape, jnp.bfloat16),
        in_specs=[VMEM] * sum(cuts),
        out_specs=ANY,
        scratch_shapes=[pltpu.SemaphoreType.DMA((sum(cuts),))],
        compiler_params=pltpu.CompilerParams(vmem_limit_bytes=8 << 20),
    )(*[p for group in parts for p in group])


def solution(mesh):
    spec = P(("grp", "blk"), None)
    return jax.shard_map(
        body, mesh=mesh, in_specs=(spec,) * 6 + (P(("grp", "blk")),), out_specs=spec, check_vma=False
    )
```

```python
import functools
import math

import jax
import jax.numpy as jnp
from jax import lax
from jax.experimental import pallas as pl
from jax.experimental.pallas import tpu as pltpu
from jax.sharding import PartitionSpec as P

KVH = 4
DH = 128
BS = 128
G = 8
GW = G * DH
ROWS = G * BS
CHUNK = 4
MAXB = 16
CHUNKS = MAXB // CHUNK
MSG = GW + 3 * DH
PLANE = 4
DEPTH = 8
WAVE = 5
NEAR = 3
SCALE = DH**-0.5 * math.log2(math.e)


def index(x, z, c):
    return ((x % 2) * 8 + z % 8) * 2 + c % 2


def pairs(target):
    return [
        (index(x, z, c), index(*target(x, z, c)))
        for x in range(2)
        for z in range(8)
        for c in range(2)
    ]


AHEAD = pairs(lambda x, z, c: (x, z + 1 - 2 * c, c))
BACK = pairs(lambda x, z, c: (x, z - 1 + 2 * c, c))
SIBLING = pairs(lambda x, z, c: (x, z, c + 1))
ACROSS = pairs(lambda x, z, c: (x + 1, z, c))
DIAGONAL = pairs(lambda x, z, c: (x + 1, z, c + 1))
PEERS = (SIBLING, ACROSS, DIAGONAL)

VMEM = pl.BlockSpec(memory_space=pltpu.VMEM)
SMEM = pl.BlockSpec(memory_space=pltpu.SMEM)
ANY = pl.BlockSpec(memory_space=pl.ANY)
HBM = pl.BlockSpec(memory_space=pltpu.HBM)


def send(piece, table):
    return lax.ppermute(piece, "blk", table)


def column(start, size):
    return pl.ds(pl.multiple_of(start * size, size), size)


def peer_heads():
    me = lax.axis_index("blk")
    x, c = me // 16, me % 2
    return [2 * x + c, 2 * x + 1 - c, 2 * (1 - x) + c, 2 * (1 - x) + 1 - c]


def mover(copies, sems):
    def move(source, target):
        copies.append(pltpu.make_async_copy(source, target, sems.at[len(copies)]))
        copies[-1].start()

    return move


def pack_pool(k_ref, v_ref, *refs):
    outs, copies = refs[:PLANE], []
    move = mover(copies, refs[PLANE])
    heads = peer_heads()
    for j in (1, 2, 3, 0):
        own = column(heads[j], DH)
        move(k_ref.at[:, own], outs[j].at[:, :DH])
        move(v_ref.at[:, own], outs[j].at[:, DH:])
    for copy in copies:
        copy.wait()


def pack_request(table_ref, length_ref, q_ref, k_ref, v_ref, *refs):
    outs, copies = refs[:PLANE], []
    move = mover(copies, refs[PLANE])
    heads = peer_heads()
    for j in (2, 3, 1, 0):
        own = column(heads[j], DH)
        move(q_ref.at[:, column(heads[j], GW)], outs[j].at[:, :GW])
        move(k_ref.at[:, own], outs[j].at[:, GW : GW + DH])
        move(v_ref.at[:, own], outs[j].at[:, GW + DH : GW + 2 * DH])
    lane = lax.broadcasted_iota(jnp.int32, (16, DH), 1)
    meta = jnp.where(lane == MAXB, length_ref[0], 0)
    for i in range(MAXB):
        meta = jnp.where(lane == i, table_ref[0, i], meta)
    meta = meta.astype(jnp.float32).astype(jnp.bfloat16)
    for j in range(PLANE):
        outs[j][:16, GW + 2 * DH :] = meta
        outs[j][16:, GW + 2 * DH :] = jnp.zeros((BS - 16, DH), jnp.bfloat16)
    for copy in copies:
        copy.wait()


def assemble(cuts, *refs):
    total = sum(cuts)
    heads = peer_heads()
    parts, out_ref, sems = refs[:total], refs[total], refs[total + 1]
    copies = []
    for j in range(PLANE):
        rows = BS // cuts[j]
        for i in range(cuts[j]):
            target = out_ref.at[i * rows : (i + 1) * rows, column(heads[j], GW)]
            at = len(copies)
            copies.append(pltpu.make_async_copy(parts[at], target, sems.at[at]))
    for copy in copies:
        copy.start()
    for copy in copies:
        copy.wait()


def attend(low, high, fresh, cuts, slot_ref, length_ref, *refs):
    n = 2
    count_pieces = high - low
    refs = list(refs)

    def take(k):
        got = refs[:k]
        del refs[:k]
        return got

    msgs, pieces = take(n), take(count_pieces)
    state = [] if fresh else take(2)
    outs = take(sum(cuts) if cuts else 2)
    kv_ref, list_ref, qs_ref, s_ref, own_ref, top_ref, acc_ref, sems = refs
    copies = [
        pltpu.make_async_copy(pieces[i], kv_ref.at[pl.ds(i * PLANE, PLANE)], sems.at[i])
        for i in range(count_pieces)
    ]
    for copy in copies:
        copy.start()
    row = lax.broadcasted_iota(jnp.int32, (ROWS, BS), 0) % BS
    causal = lax.broadcasted_iota(jnp.int32, (ROWS, BS), 1) <= row
    ones = jnp.ones((BS, DH), jnp.bfloat16)

    sizes = []
    for r in range(n):

        def pick(i, size, r=r):
            slot = slot_ref[r, i] - low * PLANE
            inside = (slot >= 0) & (slot < (high - low) * PLANE)

            @pl.when(inside)
            def _():
                list_ref[r, size] = slot

            return size + inside.astype(jnp.int32)

        sizes.append(lax.fori_loop(0, length_ref[r], pick, 0))
    count = [(size + CHUNK - 1) // CHUNK for size in sizes]

    def scores(r, keys):
        return (
            lax.dot_general(
                qs_ref[r], keys, (((1,), (1,)), ((), ())), preferred_element_type=jnp.float32
            )
            * SCALE
        )

    def begin(r):
        for h in range(G):
            qs_ref[r, h * BS : (h + 1) * BS, :] = msgs[r][:, h * DH : (h + 1) * DH]
        if fresh:
            s = jnp.where(causal, scores(r, msgs[r][:, GW : GW + DH]), -jnp.inf)
            own_ref[r] = s
            top_ref[r] = s
        else:
            top_ref[r] = state[0][r]

    def entry(r, k, j):
        at = k * CHUNK + j
        live = at < sizes[r]
        return list_ref[r, jnp.where(live, at, 0)], live

    def chunk_scores(r, k):
        keys = jnp.concatenate([kv_ref[entry(r, k, j)[0], :, :DH] for j in range(CHUNK)], axis=0)
        s = scores(r, keys)
        s_ref[r, k] = s
        top = top_ref[r]
        for j in range(CHUNK):
            top = jnp.maximum(top, s[:, j * BS : (j + 1) * BS])
        top_ref[r] = top

    def turn(r):
        top = jnp.broadcast_to(jnp.max(top_ref[r], axis=1, keepdims=True), (ROWS, BS))
        top_ref[r] = top
        if fresh:
            w = jnp.exp2(own_ref[r] - top).astype(jnp.bfloat16)
            rhs = jnp.concatenate([msgs[r][:, GW + DH : GW + 2 * DH], ones], axis=1)
            acc_ref[...] = jnp.dot(w, rhs, preferred_element_type=jnp.float32)
        else:
            acc_ref[...] = state[1][r] * jnp.tile(jnp.exp2(state[0][r] - top), (1, 2))

    def chunk_values(r, k):
        w = jnp.exp2(s_ref[r, k] - jnp.tile(top_ref[r], (1, CHUNK))).astype(jnp.bfloat16)
        rhs = []
        for j in range(CHUNK):
            slot, live = entry(r, k, j)
            both = jnp.concatenate([kv_ref[slot, :, DH:], ones], axis=1)
            rhs.append(jnp.where(live, both, jnp.zeros_like(both)))
        acc_ref[...] += jnp.dot(w, jnp.concatenate(rhs, axis=0), preferred_element_type=jnp.float32)

    def finish(r):
        if not cuts:
            outs[0][r] = top_ref[r]
            outs[1][r] = acc_ref[...]
            return
        rows = BS // cuts[r]
        for h in range(G):
            a = acc_ref[h * BS : (h + 1) * BS, :]
            a = (a[:, :DH] / a[:, DH:]).astype(jnp.bfloat16)
            for i in range(cuts[r]):
                outs[sum(cuts[:r]) + i][:, h * DH : (h + 1) * DH] = a[i * rows : (i + 1) * rows]

    begin(0)
    for copy in copies:
        copy.wait()

    @pl.loop(0, count[0])
    def _(k):
        chunk_scores(0, k)

    turn(0)
    begin(1)
    both = jnp.minimum(count[0], count[1])

    @pl.loop(0, both)
    def _(k):
        chunk_values(0, k)
        chunk_scores(1, k)

    @pl.loop(both, count[0])
    def _(k):
        chunk_values(0, k)

    @pl.loop(both, count[1])
    def _(k):
        chunk_scores(1, k)

    finish(0)
    turn(1)

    @pl.loop(0, count[1])
    def _(k):
        chunk_values(1, k)

    finish(1)


def run_attend(slots, lengths, msgs, planes, low, high, state=(), cuts=()):
    n = len(msgs)
    pieces = planes[low:high]
    chunks = min(CHUNKS, high - low)
    if cuts:
        outs = [jax.ShapeDtypeStruct((BS // cut, GW), jnp.bfloat16) for cut in cuts for _ in range(cut)]
    else:
        outs = [jax.ShapeDtypeStruct((n, ROWS, w), jnp.float32) for w in (DH, 2 * DH)]
    return pl.pallas_call(
        functools.partial(attend, low, high, not state, cuts),
        out_shape=outs,
        in_specs=[SMEM] * 2 + [VMEM] * n + [ANY] * len(pieces) + [VMEM] * len(state),
        out_specs=[VMEM] * len(outs),
        scratch_shapes=[
            pltpu.VMEM((PLANE * (high - low), BS, 2 * DH), jnp.bfloat16),
            pltpu.SMEM((n, MAXB), jnp.int32),
            pltpu.VMEM((n, ROWS, DH), jnp.bfloat16),
            pltpu.VMEM((n, chunks, ROWS, CHUNK * BS), jnp.float32),
            pltpu.VMEM((n, ROWS, BS), jnp.float32),
            pltpu.VMEM((n, ROWS, BS), jnp.float32),
            pltpu.VMEM((ROWS, 2 * DH), jnp.float32),
            pltpu.SemaphoreType.DMA((len(pieces),)),
        ],
        cost_estimate=pl.CostEstimate(flops=1, bytes_accessed=1, transcendentals=1),
        compiler_params=pltpu.CompilerParams(vmem_limit_bytes=(20 + 4 * chunks) << 20),
    )(slots, lengths, *msgs, *pieces, *state)


def body(queries, new_keys, new_values, prefix_keys, prefix_values, block_table, prefix_blocks):
    pool = pl.pallas_call(
        pack_pool,
        out_shape=[jax.ShapeDtypeStruct((BS, 2 * DH), jnp.bfloat16)] * PLANE,
        in_specs=[HBM] * 2,
        out_specs=[VMEM] * PLANE,
        scratch_shapes=[pltpu.SemaphoreType.DMA((2 * PLANE,))],
    )(prefix_keys, prefix_values)
    ahead, _ = lax.optimization_barrier((queries, pool))
    request = pl.pallas_call(
        pack_request,
        out_shape=[jax.ShapeDtypeStruct((BS, MSG), jnp.bfloat16)] * PLANE,
        in_specs=[SMEM] * 2 + [HBM] * 3,
        out_specs=[VMEM] * PLANE,
        scratch_shapes=[pltpu.SemaphoreType.DMA((3 * PLANE,))],
        cost_estimate=pl.CostEstimate(flops=1, bytes_accessed=1, transcendentals=1),
    )(block_table, prefix_blocks, ahead, new_keys, new_values)
    arrived = [pool[0]] + [send(o, t) for o, t in zip(pool[1:], PEERS)]
    arrived, request = lax.optimization_barrier((arrived, request))
    piece = jnp.stack(arrived)
    msgs = [request[0]] + [send(o, t) for o, t in zip(request[1:], PEERS)]

    me = lax.axis_index("blk")
    x, z, c = me // 16, (me // 2) % 8, me % 2

    def entries(chosen):
        info = jnp.stack([m[0, GW + 2 * DH : GW + 2 * DH + MAXB + 1] for m in chosen]).astype(jnp.int32)
        table, lengths = info[:, :MAXB], info[:, MAXB]
        deep = (((table // 2) % 8 - z) * (1 - 2 * c)) % 8
        order = jnp.where(deep < 4, jnp.maximum(2 * deep - 1, 0), jnp.minimum(2 * (8 - deep), 7))
        return order * 4 + (table // 16 ^ x) * 2 + (table % 2 ^ c), lengths

    near, far = msgs[1::-1], msgs[2:]
    slots, lengths = entries([*near, *far])
    near_work, far_work = (slots[:2], lengths[:2]), (slots[2:], lengths[2:])
    a, b = [piece], [piece]
    for _ in range(2):
        a.append(send(a[-1], AHEAD))
        b.append(send(b[-1], BACK))
    planes = [a[0], b[1], a[1], b[2], a[2]]
    near_state = run_attend(*near_work, near, planes, 0, NEAR)
    last, near_state = lax.optimization_barrier(((a[2], b[2]), near_state))
    planes += [send(last[1], BACK), send(last[0], AHEAD)]
    state = run_attend(*far_work, far, planes, 0, WAVE)
    last, state = lax.optimization_barrier((planes[-1], state))
    planes.append(send(last, AHEAD))
    state = run_attend(*far_work, far, planes, WAVE, DEPTH - 1, state)
    across, diagonal = run_attend(*far_work, far, planes, DEPTH - 1, DEPTH, state, (1, 1))
    near_state, _ = lax.optimization_barrier((near_state, diagonal))
    *sibling, mine = run_attend(*near_work, near, planes, NEAR, DEPTH, near_state, (2, 1))
    parts = [
        [mine],
        [send(p, SIBLING) for p in sibling],
        [send(p, ACROSS) for p in [across]],
        [send(p, DIAGONAL) for p in [diagonal]],
    ]
    cuts = tuple(len(p) for p in parts)
    return pl.pallas_call(
        functools.partial(assemble, cuts),
        out_shape=jax.ShapeDtypeStruct(queries.shape, jnp.bfloat16),
        in_specs=[VMEM] * sum(cuts),
        out_specs=ANY,
        scratch_shapes=[pltpu.SemaphoreType.DMA((sum(cuts),))],
        compiler_params=pltpu.CompilerParams(vmem_limit_bytes=8 << 20),
    )(*[p for group in parts for p in group])


def solution(mesh):
    spec = P(("grp", "blk"), None)
    return jax.shard_map(
        body, mesh=mesh, in_specs=(spec,) * 6 + (P(("grp", "blk")),), out_specs=spec, check_vma=False
    )
```

```python
import functools
import math

import jax
import jax.numpy as jnp
from jax import lax
from jax.experimental import pallas as pl
from jax.experimental.pallas import tpu as pltpu
from jax.sharding import PartitionSpec as P

KVH = 4
DH = 128
BS = 128
G = 8
GW = G * DH
ROWS = G * BS
CHUNK = 4
MAXB = 16
CHUNKS = MAXB // CHUNK
MSG = GW + 2 * DH
EXTRA = 16
PLANE = 4
DEPTH = 8
WAVE = 5
NEAR = 3
SCALE = DH**-0.5 * math.log2(math.e)


def index(x, z, c):
    return ((x % 2) * 8 + z % 8) * 2 + c % 2


def pairs(target):
    return [
        (index(x, z, c), index(*target(x, z, c)))
        for x in range(2)
        for z in range(8)
        for c in range(2)
    ]


AHEAD = pairs(lambda x, z, c: (x, z + 1 - 2 * c, c))
BACK = pairs(lambda x, z, c: (x, z - 1 + 2 * c, c))
SIBLING = pairs(lambda x, z, c: (x, z, c + 1))
ACROSS = pairs(lambda x, z, c: (x + 1, z, c))
DIAGONAL = pairs(lambda x, z, c: (x + 1, z, c + 1))
PEERS = (SIBLING, ACROSS, DIAGONAL)

VMEM = pl.BlockSpec(memory_space=pltpu.VMEM)
SMEM = pl.BlockSpec(memory_space=pltpu.SMEM)
ANY = pl.BlockSpec(memory_space=pl.ANY)
HBM = pl.BlockSpec(memory_space=pltpu.HBM)


def send(piece, table):
    return lax.ppermute(piece, "blk", table)


def column(start, size):
    return pl.ds(pl.multiple_of(start * size, size), size)


def peer_heads():
    me = lax.axis_index("blk")
    x, c = me // 16, me % 2
    return [2 * x + c, 2 * x + 1 - c, 2 * (1 - x) + c, 2 * (1 - x) + 1 - c]


def mover(copies, sems):
    def move(source, target):
        copies.append(pltpu.make_async_copy(source, target, sems.at[len(copies)]))
        copies[-1].start()

    return move


def pack_pool(table_ref, length_ref, k_ref, v_ref, *refs):
    outs, copies = refs[:PLANE], []
    move = mover(copies, refs[PLANE])
    heads = peer_heads()
    for j in (1, 2, 3, 0):
        own = column(heads[j], DH)
        move(k_ref.at[:, own], outs[j].at[:BS, :DH])
        move(v_ref.at[:, own], outs[j].at[:BS, DH:])
    lane = lax.broadcasted_iota(jnp.int32, (EXTRA, 2 * DH), 1)
    meta = jnp.where(lane == MAXB, length_ref[0], 0)
    for i in range(MAXB):
        meta = jnp.where(lane == i, table_ref[0, i], meta)
    meta = meta.astype(jnp.float32).astype(jnp.bfloat16)
    for j in range(PLANE):
        outs[j][BS:, :] = meta
    for copy in copies:
        copy.wait()


def pack_request(q_ref, k_ref, v_ref, *refs):
    outs, copies = refs[:PLANE], []
    move = mover(copies, refs[PLANE])
    heads = peer_heads()
    for j in (2, 3, 1, 0):
        own = column(heads[j], DH)
        move(q_ref.at[:, column(heads[j], GW)], outs[j].at[:, :GW])
        move(k_ref.at[:, own], outs[j].at[:, GW : GW + DH])
        move(v_ref.at[:, own], outs[j].at[:, GW + DH :])
    for copy in copies:
        copy.wait()


def join(*refs):
    for j in range(PLANE):
        refs[PLANE][j] = refs[j][:BS]


def assemble(cuts, *refs):
    total = sum(cuts)
    heads = peer_heads()
    parts, out_ref, sems = refs[:total], refs[total], refs[total + 1]
    copies = []
    for j in range(PLANE):
        rows = BS // cuts[j]
        for i in range(cuts[j]):
            target = out_ref.at[i * rows : (i + 1) * rows, column(heads[j], GW)]
            at = len(copies)
            copies.append(pltpu.make_async_copy(parts[at], target, sems.at[at]))
    for copy in copies:
        copy.start()
    for copy in copies:
        copy.wait()


def attend(low, high, fresh, cuts, slot_ref, length_ref, *refs):
    n = 2
    count_pieces = high - low
    refs = list(refs)

    def take(k):
        got = refs[:k]
        del refs[:k]
        return got

    msgs, pieces = take(n), take(count_pieces)
    state = [] if fresh else take(2)
    outs = take(sum(cuts) if cuts else 2)
    kv_ref, list_ref, qs_ref, s_ref, own_ref, top_ref, acc_ref, sems = refs
    copies = [
        pltpu.make_async_copy(pieces[i], kv_ref.at[pl.ds(i * PLANE, PLANE)], sems.at[i])
        for i in range(count_pieces)
    ]
    for copy in copies:
        copy.start()
    row = lax.broadcasted_iota(jnp.int32, (ROWS, BS), 0) % BS
    causal = lax.broadcasted_iota(jnp.int32, (ROWS, BS), 1) <= row
    ones = jnp.ones((BS, DH), jnp.bfloat16)

    sizes = []
    for r in range(n):

        def pick(i, size, r=r):
            slot = slot_ref[r, i] - low * PLANE
            inside = (slot >= 0) & (slot < (high - low) * PLANE)

            @pl.when(inside)
            def _():
                list_ref[r, size] = slot

            return size + inside.astype(jnp.int32)

        sizes.append(lax.fori_loop(0, length_ref[r], pick, 0))
    count = [(size + CHUNK - 1) // CHUNK for size in sizes]

    def scores(r, keys):
        return (
            lax.dot_general(
                qs_ref[r], keys, (((1,), (1,)), ((), ())), preferred_element_type=jnp.float32
            )
            * SCALE
        )

    def begin(r):
        for h in range(G):
            qs_ref[r, h * BS : (h + 1) * BS, :] = msgs[r][:, h * DH : (h + 1) * DH]
        if fresh:
            s = jnp.where(causal, scores(r, msgs[r][:, GW : GW + DH]), -jnp.inf)
            own_ref[r] = s
            top_ref[r] = s
        else:
            top_ref[r] = state[0][r]

    def entry(r, k, j):
        at = k * CHUNK + j
        live = at < sizes[r]
        return list_ref[r, jnp.where(live, at, 0)], live

    def chunk_scores(r, k):
        keys = jnp.concatenate([kv_ref[entry(r, k, j)[0], :, :DH] for j in range(CHUNK)], axis=0)
        s = scores(r, keys)
        s_ref[r, k] = s
        top = top_ref[r]
        for j in range(CHUNK):
            top = jnp.maximum(top, s[:, j * BS : (j + 1) * BS])
        top_ref[r] = top

    def turn(r):
        top = jnp.broadcast_to(jnp.max(top_ref[r], axis=1, keepdims=True), (ROWS, BS))
        top_ref[r] = top
        if fresh:
            w = jnp.exp2(own_ref[r] - top).astype(jnp.bfloat16)
            rhs = jnp.concatenate([msgs[r][:, GW + DH : GW + 2 * DH], ones], axis=1)
            acc_ref[...] = jnp.dot(w, rhs, preferred_element_type=jnp.float32)
        else:
            acc_ref[...] = state[1][r] * jnp.tile(jnp.exp2(state[0][r] - top), (1, 2))

    def chunk_values(r, k):
        w = jnp.exp2(s_ref[r, k] - jnp.tile(top_ref[r], (1, CHUNK))).astype(jnp.bfloat16)
        rhs = []
        for j in range(CHUNK):
            slot, live = entry(r, k, j)
            both = jnp.concatenate([kv_ref[slot, :, DH:], ones], axis=1)
            rhs.append(jnp.where(live, both, jnp.zeros_like(both)))
        acc_ref[...] += jnp.dot(w, jnp.concatenate(rhs, axis=0), preferred_element_type=jnp.float32)

    def finish(r):
        if not cuts:
            outs[0][r] = top_ref[r]
            outs[1][r] = acc_ref[...]
            return
        rows = BS // cuts[r]
        for h in range(G):
            a = acc_ref[h * BS : (h + 1) * BS, :]
            a = (a[:, :DH] / a[:, DH:]).astype(jnp.bfloat16)
            for i in range(cuts[r]):
                outs[sum(cuts[:r]) + i][:, h * DH : (h + 1) * DH] = a[i * rows : (i + 1) * rows]

    begin(0)
    for copy in copies:
        copy.wait()

    @pl.loop(0, count[0])
    def _(k):
        chunk_scores(0, k)

    turn(0)
    begin(1)
    both = jnp.minimum(count[0], count[1])

    @pl.loop(0, both)
    def _(k):
        chunk_values(0, k)
        chunk_scores(1, k)

    @pl.loop(both, count[0])
    def _(k):
        chunk_values(0, k)

    @pl.loop(both, count[1])
    def _(k):
        chunk_scores(1, k)

    finish(0)
    turn(1)

    @pl.loop(0, count[1])
    def _(k):
        chunk_values(1, k)

    finish(1)


def run_attend(slots, lengths, msgs, planes, low, high, state=(), cuts=()):
    n = len(msgs)
    pieces = planes[low:high]
    chunks = min(CHUNKS, high - low)
    if cuts:
        outs = [jax.ShapeDtypeStruct((BS // cut, GW), jnp.bfloat16) for cut in cuts for _ in range(cut)]
    else:
        outs = [jax.ShapeDtypeStruct((n, ROWS, w), jnp.float32) for w in (DH, 2 * DH)]
    return pl.pallas_call(
        functools.partial(attend, low, high, not state, cuts),
        out_shape=outs,
        in_specs=[SMEM] * 2 + [VMEM] * n + [ANY] * len(pieces) + [VMEM] * len(state),
        out_specs=[VMEM] * len(outs),
        scratch_shapes=[
            pltpu.VMEM((PLANE * (high - low), BS, 2 * DH), jnp.bfloat16),
            pltpu.SMEM((n, MAXB), jnp.int32),
            pltpu.VMEM((n, ROWS, DH), jnp.bfloat16),
            pltpu.VMEM((n, chunks, ROWS, CHUNK * BS), jnp.float32),
            pltpu.VMEM((n, ROWS, BS), jnp.float32),
            pltpu.VMEM((n, ROWS, BS), jnp.float32),
            pltpu.VMEM((ROWS, 2 * DH), jnp.float32),
            pltpu.SemaphoreType.DMA((len(pieces),)),
        ],
        cost_estimate=pl.CostEstimate(flops=1, bytes_accessed=1, transcendentals=1),
        compiler_params=pltpu.CompilerParams(vmem_limit_bytes=(20 + 4 * chunks) << 20),
    )(slots, lengths, *msgs, *pieces, *state)


def body(queries, new_keys, new_values, prefix_keys, prefix_values, block_table, prefix_blocks):
    pool = pl.pallas_call(
        pack_pool,
        out_shape=[jax.ShapeDtypeStruct((BS + EXTRA, 2 * DH), jnp.bfloat16)] * PLANE,
        in_specs=[SMEM] * 2 + [HBM] * 2,
        out_specs=[VMEM] * PLANE,
        scratch_shapes=[pltpu.SemaphoreType.DMA((2 * PLANE,))],
    )(block_table, prefix_blocks, prefix_keys, prefix_values)
    ahead, _ = lax.optimization_barrier((queries, pool))
    request = pl.pallas_call(
        pack_request,
        out_shape=[jax.ShapeDtypeStruct((BS, MSG), jnp.bfloat16)] * PLANE,
        in_specs=[HBM] * 3,
        out_specs=[VMEM] * PLANE,
        scratch_shapes=[pltpu.SemaphoreType.DMA((3 * PLANE,))],
        cost_estimate=pl.CostEstimate(flops=1, bytes_accessed=1, transcendentals=1),
    )(ahead, new_keys, new_values)
    arrived = [pool[0]] + [send(o, t) for o, t in zip(pool[1:], PEERS)]
    arrived, request = lax.optimization_barrier((arrived, request))
    piece = pl.pallas_call(
        join,
        out_shape=jax.ShapeDtypeStruct((PLANE, BS, 2 * DH), jnp.bfloat16),
        in_specs=[VMEM] * PLANE,
        out_specs=VMEM,
        cost_estimate=pl.CostEstimate(flops=1, bytes_accessed=1, transcendentals=1),
        compiler_params=pltpu.CompilerParams(vmem_limit_bytes=8 << 20),
    )(*arrived)
    msgs = [request[0]] + [send(o, t) for o, t in zip(request[1:], PEERS)]

    me = lax.axis_index("blk")
    x, z, c = me // 16, (me // 2) % 8, me % 2

    def entries(chosen):
        info = jnp.stack([m[BS, : MAXB + 1] for m in chosen]).astype(jnp.int32)
        table, lengths = info[:, :MAXB], info[:, MAXB]
        deep = (((table // 2) % 8 - z) * (1 - 2 * c)) % 8
        order = jnp.where(deep < 4, jnp.maximum(2 * deep - 1, 0), jnp.minimum(2 * (8 - deep), 7))
        return order * 4 + (table // 16 ^ x) * 2 + (table % 2 ^ c), lengths

    near, far = msgs[1::-1], msgs[2:]
    slots, lengths = entries([arrived[1], arrived[0], arrived[2], arrived[3]])
    near_work, far_work = (slots[:2], lengths[:2]), (slots[2:], lengths[2:])
    a, b = [piece], [piece]
    for _ in range(2):
        a.append(send(a[-1], AHEAD))
        b.append(send(b[-1], BACK))
    planes = [a[0], b[1], a[1], b[2], a[2]]
    near_state = run_attend(*near_work, near, planes, 0, NEAR)
    last, near_state = lax.optimization_barrier(((a[2], b[2]), near_state))
    planes += [send(last[1], BACK), send(last[0], AHEAD)]
    state = run_attend(*far_work, far, planes, 0, WAVE)
    last, state = lax.optimization_barrier((planes[-1], state))
    planes.append(send(last, AHEAD))
    state = run_attend(*far_work, far, planes, WAVE, DEPTH - 1, state)
    across, diagonal = run_attend(*far_work, far, planes, DEPTH - 1, DEPTH, state, (1, 1))
    near_state, _ = lax.optimization_barrier((near_state, diagonal))
    *sibling, mine = run_attend(*near_work, near, planes, NEAR, DEPTH, near_state, (2, 1))
    parts = [
        [mine],
        [send(p, SIBLING) for p in sibling],
        [send(p, ACROSS) for p in [across]],
        [send(p, DIAGONAL) for p in [diagonal]],
    ]
    cuts = tuple(len(p) for p in parts)
    return pl.pallas_call(
        functools.partial(assemble, cuts),
        out_shape=jax.ShapeDtypeStruct(queries.shape, jnp.bfloat16),
        in_specs=[VMEM] * sum(cuts),
        out_specs=ANY,
        scratch_shapes=[pltpu.SemaphoreType.DMA((sum(cuts),))],
        compiler_params=pltpu.CompilerParams(vmem_limit_bytes=8 << 20),
    )(*[p for group in parts for p in group])


def solution(mesh):
    spec = P(("grp", "blk"), None)
    return jax.shard_map(
        body, mesh=mesh, in_specs=(spec,) * 6 + (P(("grp", "blk")),), out_specs=spec, check_vma=False
    )
```
